32 devices in a mesh: blk: 8 (over z, x), task: 4 (over y, core).
Axes of the slice: x: 2, y: 2, z: 4, core: 2. Of those that a mesh axis runs over, the one named last changes fastest.
Arguments:
- amplitudes: bfloat16 [1024, 1024, 128], P('blk', 'task'), may hold values from -6 to 6
- integral_tiles: bfloat16 [8, 4, 4, 2, 1024, 128], P('blk', 'task'), may hold values from -0.09375 to 0.09375
- task_list: int32 [8, 4, 4, 2], P(None, 'task'), may hold values from 0 to 255
- block_offsets: int32 [8, 4, 4, 2], P(None, 'task'), may hold values from 0 to 15
- tile_counts: int32 [8, 4, 4], P(None, 'task'), may hold values from 1 to 2, as said below
Outputs:
- ladder: float32 [128, 2048], P('blk', 'task')
The draws below stay inside these ranges and needn't reach their ends.
Inputs may be any that keep to these rules, and one draw needn't show every extreme that they name: `tile_counts`: in each blk group exactly one worker receives 2 live tiles from every producer of that group, and every other worker receives exactly 1 live tile from each producer.
All inputs are finite; a program needn't handle non-finite values.
Results may differ from the reference program's by a relative error of at most 0.0003.
Values may be sent and summed in bfloat16 or wider, within the bound.
No kernel may reach another device: no remote copies, remote signals or barrier semaphores. Data moves between devices by JAX's collectives and lax.ppermute only.
A program may use at most 128 MiB of HBM per device.

```python
import jax
import jax.numpy as jnp
from jax import lax

NV = 1024
P_SIZE = 128
RB = 128
NRB = 16
CAP = 2
N_BLK = 8
N_TASK = 4


def draw_tile_counts(key, part):
    base_counts = jax.random.randint(jax.random.fold_in(key, 11), (N_BLK, N_TASK, N_TASK), 1, CAP // 2 + 1)
    busy_worker = jax.random.randint(jax.random.fold_in(key, 12), (N_BLK,), 0, N_TASK)
    is_busy = jnp.arange(N_TASK)[None, None, :] == busy_worker[:, None, None]
    return jnp.where(is_busy, CAP, base_counts).astype(jnp.int32)


def plant(array, own_key, smallest, top_value):
    shape = array.shape
    spot = [jax.random.randint(jax.random.fold_in(own_key, axis), (), 0, shape[axis]) for axis in range(len(shape))]
    array = array.at[tuple(spot)].set(smallest)
    longest = shape.index(max(shape))
    spot[longest] = (spot[longest] + 1) % shape[longest]
    return array.at[tuple(spot)].set(top_value)


def shard_levels(key, dims, split, least, largest):
    level, own = 1.0, jax.random.fold_in(key, 6)
    for dim, blocks in split:
        heights = jnp.exp(jax.random.uniform(jax.random.fold_in(own, dim), (blocks,), jnp.float32, least / len(split), largest / len(split)))
        level = level * jnp.repeat(heights, dims[dim] // blocks).reshape([-1 if axis == dim else 1 for axis in range(len(dims))])
    return level


def bell_draw(key, dims, spread, bound, cuts=(), kind=jnp.bfloat16):
    result = jax.random.normal(key, dims, jnp.float32) * spread
    if len(cuts) > 0:
        result = shard_levels(key, dims, cuts, -0.22, 0.18) * result
    return jnp.clip(result, min=-bound, max=bound).astype(kind)


def setup_inputs(seed: int = 0) -> dict:
    keys = jax.random.split(jax.random.key(seed), 6)
    amplitudes = bell_draw(keys[0], (NV, NV, P_SIZE), 1.0, 6.0, ((0, 8), (1, 4)))
    integral_tiles = bell_draw(keys[1], (N_BLK, N_TASK, N_TASK, CAP, NV, RB), (NV * N_BLK * N_TASK * CAP // NRB) ** -0.5, 0.09375, ((0, 8), (1, 4)))
    task_list = plant(jax.random.randint(keys[2], (N_BLK, N_TASK, N_TASK, CAP), 0, NV // N_TASK), jax.random.fold_in(keys[2], 1), 0, (NV // N_TASK) - 1).astype(jnp.int32)
    block_offsets = plant(jax.random.randint(keys[3], (N_BLK, N_TASK, N_TASK, CAP), 0, NRB), jax.random.fold_in(keys[3], 1), 0, NRB - 1).astype(jnp.int32)
    tile_counts = draw_tile_counts(jax.random.fold_in(keys[5], 71), 0)
    return {"amplitudes": amplitudes, "integral_tiles": integral_tiles, "task_list": task_list, "block_offsets": block_offsets, "tile_counts": tile_counts}


def reference(amplitudes, integral_tiles, task_list, block_offsets, tile_counts):
    column_span = NV // N_TASK
    slot_total = N_TASK * CAP
    column_base = (jnp.arange(N_TASK, dtype=jnp.int32) * column_span)[:, None]
    slot_rank = jnp.arange(CAP, dtype=jnp.int32)[None, :]
    block_ids = jnp.arange(NRB, dtype=jnp.int32)[None, :]

    def one_producer(residual, producer):
        blk_group = producer // N_TASK
        task_worker = producer % N_TASK
        tile_set = integral_tiles[blk_group, task_worker].reshape(slot_total, NV, RB).astype(jnp.float32)
        columns = (column_base + task_list[blk_group, task_worker]).reshape(-1).astype(jnp.int32)
        live_mask = (slot_rank < tile_counts[blk_group, task_worker][:, None]).reshape(-1)
        matched = (block_offsets[blk_group, task_worker].reshape(-1)[:, None] == block_ids) & live_mask[:, None]
        placement = jnp.where(matched, 1.0, 0.0).astype(jnp.float32)
        picked = jnp.take(amplitudes, columns, axis=1).astype(jnp.float32)
        products = jnp.einsum("cnp,ncr->npr", picked, tile_set, precision=lax.Precision.HIGHEST)
        added = jnp.einsum("nb,npr->pbr", placement, products, precision=lax.Precision.HIGHEST)
        return residual + added, None

    start = jnp.zeros((P_SIZE, NRB, RB), jnp.float32)
    residual, _ = lax.scan(one_producer, start, jnp.arange(N_BLK * N_TASK, dtype=jnp.int32))
    return residual.reshape(P_SIZE, NRB * RB)
```

```python
import functools

import jax
import jax.numpy as jnp
from jax import lax
from jax.experimental import pallas as pl
from jax.experimental.pallas import tpu as pltpu
from jax.sharding import Mesh, PartitionSpec as P

NRB = 16
TASK = ("ty", "core")
EVERY = ("blk", "ty", "core")


def ladder_kernel(meta, columns, tiles, keep, send, total, *, group, row_tasks, pair_blocks):
    step = pl.program_id(0)
    slots = pl.num_programs(0) * group

    @pl.when(step == 0)
    def _():
        total[...] = jnp.zeros_like(total)

    def add_slot(n, carry):
        slot = step * group + n

        @pl.when(meta[slots + slot] > 0)
        def _():
            product = lax.dot_general(
                columns[n], tiles[n], (((0,), (0,)), ((), ())), preferred_element_type=jnp.float32
            )
            total[meta[slot]] += product

        return carry

    lax.fori_loop(0, group, add_slot, 0, unroll=True)

    @pl.when(step == pl.num_programs(0) - 1)
    def _():
        core = meta[2 * slots]
        rows = NRB // (2 * row_tasks)
        pairs = total.shape[1] // pair_blocks
        for task in range(row_tasks):
            for block in range(pair_blocks):
                span = pl.ds(block * pairs, pairs)
                for row in range(rows):
                    keep[block, task, row] = total[(2 * task + core) * rows + row, span, :]
                    send[block, task, row] = total[(2 * task + 1 - core) * rows + row, span, :]


def body(amplitudes, integral_tiles, task_list, block_offsets, tile_counts, *, shape):
    blocks, row_tasks = shape
    tasks = 2 * row_tasks
    chunk, _, pair_total = amplitudes.shape
    capacity, row_block = integral_tiles.shape[3], integral_tiles.shape[5]
    slots = blocks * tasks * capacity

    cut = integral_tiles.reshape(tasks, capacity, blocks, chunk, row_block)
    cut = jnp.transpose(cut, (2, 0, 1, 3, 4)).reshape(blocks * tasks, capacity, chunk, row_block)
    arrived = lax.all_to_all(cut, EVERY, 0, 0, tiled=True).reshape(slots, chunk, row_block)

    rank = jnp.arange(capacity, dtype=jnp.int32)
    live = (rank < tile_counts[..., None]).astype(jnp.int32)
    packed = (task_list * NRB + block_offsets) * 2 + live
    lists = lax.all_gather(packed, TASK, axis=1, tiled=True)
    core = lax.axis_index("core").astype(jnp.int32)
    worker = lax.axis_index("ty") * 2 + core
    mine = lax.dynamic_index_in_dim(lists, worker, 2, keepdims=False).reshape(slots)
    column = mine // (2 * NRB)
    meta = jnp.concatenate([(mine // 2) % NRB, mine % 2, core[None]])
    picked = jnp.take(jnp.transpose(amplitudes, (1, 0, 2)), column, axis=0, mode="clip")

    group = 8
    rows, pairs = NRB // tasks, pair_total // blocks
    part = jax.ShapeDtypeStruct((blocks, row_tasks, rows, pairs, row_block), jnp.float32)
    whole = pl.BlockSpec(part.shape, lambda i, m: (0,) * 5)
    keep, send = pl.pallas_call(
        functools.partial(ladder_kernel, group=group, row_tasks=row_tasks, pair_blocks=blocks),
        out_shape=(part, part),
        grid_spec=pltpu.PrefetchScalarGridSpec(
            num_scalar_prefetch=1,
            grid=(slots // group,),
            in_specs=[
                pl.BlockSpec((group, chunk, pair_total), lambda i, m: (i, 0, 0)),
                pl.BlockSpec((group, chunk, row_block), lambda i, m: (i, 0, 0)),
            ],
            out_specs=(whole, whole),
            scratch_shapes=[pltpu.VMEM((NRB, pair_total, row_block), jnp.float32)],
        ),
        compiler_params=pltpu.CompilerParams(vmem_limit_bytes=24 << 20),
        cost_estimate=pl.CostEstimate(
            flops=2 * slots * chunk * pair_total * row_block,
            bytes_accessed=2 * slots * chunk * (pair_total + row_block) + 8 * NRB * pair_total * row_block,
            transcendentals=0,
        ),
        name="ladder",
    )(meta, picked, arrived)

    other = lax.ppermute(send, "core", [(0, 1), (1, 0)])
    half = (keep + other).reshape(blocks * row_tasks, rows, pairs, row_block)
    parts = lax.all_to_all(half, ("blk", "ty"), 0, 0, tiled=True)
    out = jnp.sum(parts, axis=0)
    return jnp.transpose(out, (1, 0, 2)).reshape(pairs, rows * row_block)


def solution(mesh):
    blocks, tasks = mesh.shape["blk"], mesh.shape["task"]
    fine = Mesh(mesh.devices.reshape(blocks, tasks // 2, 2), EVERY)
    placed = (
        P("blk", TASK, None),
        P("blk", TASK, None, None, None, None),
        P(None, TASK, None, None),
        P(None, TASK, None, None),
        P(None, TASK, None),
    )
    return jax.shard_map(
        functools.partial(body, shape=(blocks, tasks // 2)),
        mesh=fine, in_specs=placed, out_specs=P("blk", TASK), check_vma=False,
    )
```

```python
import functools

import jax
import jax.numpy as jnp
from jax import lax
from jax.experimental import pallas as pl
from jax.experimental.pallas import tpu as pltpu
from jax.sharding import Mesh, PartitionSpec as P

NRB = 16
TASK = ("ty", "core")
EVERY = ("blk", "ty", "core")


def pack_kernel(busy, first, second, out):
    chunk = first.shape[1]
    out[:, :chunk] = first[...]
    out[:, chunk:] = second[...]


def pack(integral_tiles, busy, blocks):
    tasks, _, virt_total, row_block = integral_tiles.shape[2:]
    chunk = virt_total // blocks
    piece = chunk // tasks
    flat = integral_tiles.reshape(tasks * 2, blocks, chunk, row_block)
    pieces = integral_tiles.reshape(tasks * 2, blocks, tasks, piece, row_block)
    return pl.pallas_call(
        pack_kernel,
        out_shape=jax.ShapeDtypeStruct((blocks, tasks, chunk + piece, row_block), flat.dtype),
        grid_spec=pltpu.PrefetchScalarGridSpec(
            num_scalar_prefetch=1,
            grid=(tasks,),
            in_specs=[
                pl.BlockSpec((None, blocks, chunk, row_block), lambda w, m: (2 * w, 0, 0, 0)),
                pl.BlockSpec((None, blocks, None, piece, row_block), lambda w, m: (2 * m[0] + 1, 0, w, 0, 0)),
            ],
            out_specs=pl.BlockSpec((blocks, None, chunk + piece, row_block), lambda w, m: (0, w, 0, 0)),
        ),
        compiler_params=pltpu.CompilerParams(vmem_limit_bytes=8 << 20),
        name="pack",
    )(busy, flat, pieces)


def ladder_kernel(meta, columns, extras, tiles, keep, send, total, *, row_tasks, pair_blocks):
    slots, _, chunk = columns.shape
    total[...] = jnp.zeros_like(total)

    def add_slots(step, carry):
        for part in range(4):
            n = step * 4 + part
            total[meta[n]] += jnp.dot(columns[n], tiles[n, :chunk], preferred_element_type=jnp.float32)
            total[meta[slots + n]] += jnp.dot(extras[n], tiles[n, chunk:], preferred_element_type=jnp.float32)
        return carry

    lax.fori_loop(0, slots // 4, add_slots, 0)

    core = meta[2 * slots]
    rows = NRB // (2 * row_tasks)
    pairs = total.shape[1] // pair_blocks
    for task in range(row_tasks):
        for block in range(pair_blocks):
            span = pl.ds(block * pairs, pairs)
            for row in range(rows):
                keep[block, task, row] = total[(2 * task + core) * rows + row, span, :]
                send[block, task, row] = total[(2 * task + 1 - core) * rows + row, span, :]


def body(amplitudes, integral_tiles, task_list, block_offsets, tile_counts, *, shape):
    blocks, row_tasks = shape
    tasks = 2 * row_tasks
    chunk, span, pair_total = amplitudes.shape
    row_block = integral_tiles.shape[5]
    slots = blocks * tasks
    piece = chunk // tasks
    rows, pairs = NRB // tasks, pair_total // blocks
    core = lax.axis_index("core").astype(jnp.int32)
    ty = lax.axis_index("ty").astype(jnp.int32)
    worker = ty * 2 + core

    busy = jnp.argmax(tile_counts[:, 0], axis=-1).astype(jnp.int32)
    own = lax.dynamic_slice_in_dim(busy, lax.axis_index("blk"), 1)
    sent = pack(integral_tiles, own, blocks).reshape(slots, chunk + piece, row_block)
    arrived = lax.all_to_all(sent, EVERY, 0, 0, tiled=True)

    lists = lax.all_gather(task_list * NRB + block_offsets, TASK, axis=1, tiled=True)
    mine = lax.dynamic_index_in_dim(lists, worker, 2, keepdims=False)
    is_busy = busy[:, None, None] == jnp.arange(tasks, dtype=jnp.int32)
    second_row = jnp.sum(jnp.where(is_busy, lists[..., 1] % NRB, 0), axis=-1)
    meta = jnp.concatenate([(mine[..., 0] % NRB).reshape(-1), second_row.reshape(-1), core[None]])

    virt = jnp.arange(span, dtype=jnp.int32)
    owner = (busy == worker)[:, None, None]
    hot = ((mine[..., 1] // NRB)[..., None] == virt) & owner
    held = jnp.einsum("nd,cdp->cnp", hot.reshape(slots, span).astype(amplitudes.dtype), amplitudes)
    held = held.reshape(row_tasks, 2, piece, slots, pair_total)
    here = lax.dynamic_index_in_dim(held, core, 1, keepdims=False)
    there = lax.dynamic_index_in_dim(held, 1 - core, 1, keepdims=False)
    merged = here + lax.ppermute(there, "core", [(0, 1), (1, 0)])
    extras = lax.dynamic_index_in_dim(merged, ty, 0, keepdims=False)
    for hop in range(1, row_tasks):
        away = lax.dynamic_index_in_dim(merged, lax.rem(ty + hop, row_tasks), 0, keepdims=False)
        extras += lax.ppermute(away, "ty", [(i, (i + hop) % row_tasks) for i in range(row_tasks)])
    extras = jnp.transpose(extras, (1, 2, 0))

    hot = (mine[..., 0] // NRB)[..., None] == virt
    columns = jnp.einsum("nd,cdp->npc", hot.reshape(slots, span).astype(amplitudes.dtype), amplitudes)

    part = jax.ShapeDtypeStruct((blocks, row_tasks, rows, pairs, row_block), jnp.float32)
    in_vmem = pl.BlockSpec(memory_space=pltpu.VMEM)
    keep, send = pl.pallas_call(
        functools.partial(ladder_kernel, row_tasks=row_tasks, pair_blocks=blocks),
        out_shape=(part, part),
        in_specs=[pl.BlockSpec(memory_space=pltpu.SMEM), in_vmem, in_vmem, in_vmem],
        out_specs=(in_vmem, in_vmem),
        scratch_shapes=[pltpu.VMEM((NRB, pair_total, row_block), jnp.float32)],
        compiler_params=pltpu.CompilerParams(vmem_limit_bytes=16 << 20),
        cost_estimate=pl.CostEstimate(
            flops=2 * slots * (chunk + piece) * pair_total * row_block,
            bytes_accessed=2 * slots * (chunk + piece) * (pair_total + row_block) + 4 * NRB * pair_total * row_block,
            transcendentals=0,
        ),
        name="ladder",
    )(meta, columns, extras, arrived)

    other = lax.ppermute(send, "core", [(0, 1), (1, 0)])
    half = (keep + other).reshape(blocks * row_tasks, rows, pairs, row_block)
    parts = lax.all_to_all(half, ("blk", "ty"), 0, 0, tiled=True)
    out = jnp.sum(parts, axis=0)
    return jnp.transpose(out, (1, 0, 2)).reshape(pairs, rows * row_block)


def solution(mesh):
    blocks, tasks = mesh.shape["blk"], mesh.shape["task"]
    fine = Mesh(mesh.devices.reshape(blocks, tasks // 2, 2), EVERY)
    placed = (
        P("blk", TASK, None),
        P("blk", TASK, None, None, None, None),
        P(None, TASK, None, None),
        P(None, TASK, None, None),
        P(None, TASK, None),
    )
    return jax.shard_map(
        functools.partial(body, shape=(blocks, tasks // 2)),
        mesh=fine, in_specs=placed, out_specs=P("blk", TASK), check_vma=False,
    )
```

```python
import functools

import jax
import jax.numpy as jnp
from jax import lax
from jax.experimental import pallas as pl
from jax.experimental.pallas import tpu as pltpu
from jax.sharding import Mesh, PartitionSpec as P

NRB = 16
TASK = ("ty", "core")
EVERY = ("blk", "ty", "core")


def pack_kernel(counts, tiles, pieces, out, first_sem, second_sem):
    blocks, tasks, _, _ = out.shape
    chunk = tiles.shape[2]
    copies = [
        pltpu.make_async_copy(tiles.at[2 * w], out.at[:, w, pl.ds(0, chunk)], first_sem.at[w])
        for w in range(tasks)
    ]
    for copy in copies:
        copy.start()
    group = lax.axis_index("blk")
    second = 1
    for w in range(1, tasks):
        second = jnp.where(counts[w, group] == 2, 2 * w + 1, second)
    more = [
        pltpu.make_async_copy(
            pieces.at[second, :, w], out.at[:, w, pl.ds(chunk, pieces.shape[3])], second_sem.at[w]
        )
        for w in range(tasks)
    ]
    for copy in more:
        copy.start()
    for copy in copies + more:
        copy.wait()


def pack(integral_tiles, tile_counts, blocks):
    tasks, _, virt_total, row_block = integral_tiles.shape[2:]
    chunk = virt_total // blocks
    piece = chunk // tasks
    tiles = integral_tiles.reshape(tasks * 2, blocks, chunk, row_block)
    pieces = integral_tiles.reshape(tasks * 2, blocks, tasks, piece, row_block)
    counts = jnp.transpose(tile_counts[:, 0])
    if piece % 16:
        own = lax.dynamic_index_in_dim(counts, lax.axis_index("blk"), 1, keepdims=False)
        second = lax.dynamic_index_in_dim(pieces, 2 * jnp.argmax(own) + 1, 0, keepdims=False)
        return jnp.concatenate([jnp.swapaxes(tiles[::2], 0, 1), second], axis=2)
    return pl.pallas_call(
        pack_kernel,
        out_shape=jax.ShapeDtypeStruct((blocks, tasks, chunk + piece, row_block), tiles.dtype),
        in_specs=[
            pl.BlockSpec(memory_space=pltpu.SMEM),
            pl.BlockSpec(memory_space=pl.ANY),
            pl.BlockSpec(memory_space=pl.ANY),
        ],
        out_specs=pl.BlockSpec(memory_space=pltpu.VMEM),
        scratch_shapes=[pltpu.SemaphoreType.DMA((tasks,)), pltpu.SemaphoreType.DMA((tasks,))],
        compiler_params=pltpu.CompilerParams(vmem_limit_bytes=8 << 20),
        name="pack",
    )(counts, tiles, pieces)


def ladder_kernel(meta, columns, extras, tiles, keep, send, total, *, row_tasks, pair_blocks):
    slots, _, chunk = columns.shape
    total[...] = jnp.zeros_like(total)

    def add_slots(step, carry):
        for part in range(4):
            n = step * 4 + part
            total[meta[n]] += jnp.dot(columns[n], tiles[n, :chunk], preferred_element_type=jnp.float32)
            total[meta[slots + n]] += jnp.dot(extras[n], tiles[n, chunk:], preferred_element_type=jnp.float32)
        return carry

    lax.fori_loop(0, slots // 4, add_slots, 0)

    core = meta[2 * slots]
    rows = NRB // (2 * row_tasks)
    pairs = total.shape[1] // pair_blocks
    for task in range(row_tasks):
        for block in range(pair_blocks):
            span = pl.ds(block * pairs, pairs)
            for row in range(rows):
                keep[block, task, row] = total[(2 * task + core) * rows + row, span, :]
                send[block, task, row] = total[(2 * task + 1 - core) * rows + row, span, :]


def body(amplitudes, integral_tiles, task_list, block_offsets, tile_counts, *, shape):
    blocks, row_tasks = shape
    tasks = 2 * row_tasks
    chunk, span, pair_total = amplitudes.shape
    row_block = integral_tiles.shape[5]
    slots = blocks * tasks
    piece = chunk // tasks
    rows, pairs = NRB // tasks, pair_total // blocks
    core = lax.axis_index("core").astype(jnp.int32)
    ty = lax.axis_index("ty").astype(jnp.int32)
    worker = ty * 2 + core

    busy = jnp.argmax(tile_counts[:, 0], axis=-1).astype(jnp.int32)
    sent = pack(integral_tiles, tile_counts, blocks).reshape(slots, chunk + piece, row_block)
    arrived = lax.all_to_all(sent, EVERY, 0, 0, tiled=True)

    lists = lax.all_gather(task_list * NRB + block_offsets, TASK, axis=1, tiled=True)
    mine = lax.dynamic_index_in_dim(lists, worker, 2, keepdims=False)
    is_busy = busy[:, None, None] == jnp.arange(tasks, dtype=jnp.int32)
    second_row = jnp.sum(jnp.where(is_busy, lists[..., 1] % NRB, 0), axis=-1)
    meta = jnp.concatenate([(mine[..., 0] % NRB).reshape(-1), second_row.reshape(-1), core[None]])

    virt = jnp.arange(span, dtype=jnp.int32)
    owner = (busy == worker)[:, None, None]
    hot = ((mine[..., 1] // NRB)[..., None] == virt) & owner
    held = jnp.einsum("nd,cdp->cnp", hot.reshape(slots, span).astype(amplitudes.dtype), amplitudes)
    held = held.reshape(row_tasks, 2, piece, slots, pair_total)
    here = lax.dynamic_index_in_dim(held, core, 1, keepdims=False)
    there = lax.dynamic_index_in_dim(held, 1 - core, 1, keepdims=False)
    merged = here + lax.ppermute(there, "core", [(0, 1), (1, 0)])
    extras = lax.dynamic_index_in_dim(merged, ty, 0, keepdims=False)
    for hop in range(1, row_tasks):
        away = lax.dynamic_index_in_dim(merged, lax.rem(ty + hop, row_tasks), 0, keepdims=False)
        extras += lax.ppermute(away, "ty", [(i, (i + hop) % row_tasks) for i in range(row_tasks)])
    extras = jnp.transpose(extras, (1, 2, 0))

    first = mine[..., 0] // NRB
    first, _ = lax.optimization_barrier((first, merged))
    hot = first[..., None] == virt
    columns = jnp.einsum("nd,cdp->npc", hot.reshape(slots, span).astype(amplitudes.dtype), amplitudes)

    part = jax.ShapeDtypeStruct((blocks, row_tasks, rows, pairs, row_block), jnp.float32)
    in_vmem = pl.BlockSpec(memory_space=pltpu.VMEM)
    keep, send = pl.pallas_call(
        functools.partial(ladder_kernel, row_tasks=row_tasks, pair_blocks=blocks),
        out_shape=(part, part),
        in_specs=[pl.BlockSpec(memory_space=pltpu.SMEM), in_vmem, in_vmem, in_vmem],
        out_specs=(in_vmem, in_vmem),
        scratch_shapes=[pltpu.VMEM((NRB, pair_total, row_block), jnp.float32)],
        compiler_params=pltpu.CompilerParams(vmem_limit_bytes=16 << 20),
        cost_estimate=pl.CostEstimate(
            flops=2 * slots * (chunk + piece) * pair_total * row_block,
            bytes_accessed=2 * slots * (chunk + piece) * (pair_total + row_block) + 4 * NRB * pair_total * row_block,
            transcendentals=0,
        ),
        name="ladder",
    )(meta, columns, extras, arrived)

    other = lax.ppermute(send, "core", [(0, 1), (1, 0)])
    half = (keep + other).reshape(blocks * row_tasks, rows, pairs, row_block)
    parts = lax.all_to_all(half, ("blk", "ty"), 0, 0, tiled=True)
    out = jnp.sum(parts, axis=0)
    return jnp.transpose(out, (1, 0, 2)).reshape(pairs, rows * row_block)


def solution(mesh):
    blocks, tasks = mesh.shape["blk"], mesh.shape["task"]
    fine = Mesh(mesh.devices.reshape(blocks, tasks // 2, 2), EVERY)
    placed = (
        P("blk", TASK, None),
        P("blk", TASK, None, None, None, None),
        P(None, TASK, None, None),
        P(None, TASK, None, None),
        P(None, TASK, None),
    )
    return jax.shard_map(
        functools.partial(body, shape=(blocks, tasks // 2)),
        mesh=fine, in_specs=placed, out_specs=P("blk", TASK), check_vma=False,
    )
```

```python
import functools

import jax
import jax.numpy as jnp
from jax import lax
from jax.experimental import pallas as pl
from jax.experimental.pallas import tpu as pltpu
from jax.sharding import Mesh, PartitionSpec as P

NRB = 16
TASK = ("ty", "core")
EVERY = ("blk", "ty", "core")


def pack_kernel(counts, tiles, pieces, out, held, busy, first_sem, second_sem, out_sem, count_sem):
    tasks, _, rows, _ = held.shape
    chunk = tiles.shape[2]
    count_copy = pltpu.make_async_copy(counts, busy, count_sem)
    count_copy.start()
    first = [
        pltpu.make_async_copy(tiles.at[2 * w], held.at[w, :, pl.ds(0, chunk)], first_sem.at[w])
        for w in range(tasks)
    ]
    for copy in first:
        copy.start()
    count_copy.wait()
    group = lax.axis_index("blk")
    tile = 1
    for w in range(1, tasks):
        tile = jnp.where(busy[w, group] == 2, 2 * w + 1, tile)
    second = [
        pltpu.make_async_copy(pieces.at[tile, :, w], held.at[w, :, pl.ds(chunk, rows - chunk)], second_sem.at[w])
        for w in range(tasks)
    ]
    for copy in second:
        copy.start()
    leave = [pltpu.make_async_copy(held.at[w], out.at[:, w], out_sem.at[w]) for w in range(tasks)]
    for w in range(tasks):
        first[w].wait()
        second[w].wait()
        leave[w].start()
    for copy in leave:
        copy.wait()


def pack(integral_tiles, tile_counts, blocks):
    tasks, _, virt_total, row_block = integral_tiles.shape[2:]
    chunk = virt_total // blocks
    piece = chunk // tasks
    tiles = integral_tiles.reshape(tasks * 2, blocks, chunk, row_block)
    pieces = integral_tiles.reshape(tasks * 2, blocks, tasks, piece, row_block)
    counts = jnp.transpose(tile_counts[:, 0])
    if piece % 16:
        own = lax.dynamic_index_in_dim(counts, lax.axis_index("blk"), 1, keepdims=False)
        second = lax.dynamic_index_in_dim(pieces, 2 * jnp.argmax(own) + 1, 0, keepdims=False)
        return jnp.concatenate([jnp.swapaxes(tiles[::2], 0, 1), second], axis=2)
    return pl.pallas_call(
        pack_kernel,
        out_shape=jax.ShapeDtypeStruct((blocks, tasks, chunk + piece, row_block), tiles.dtype),
        in_specs=[pl.BlockSpec(memory_space=pl.ANY)] * 3,
        out_specs=pl.BlockSpec(memory_space=pl.ANY),
        scratch_shapes=[
            pltpu.VMEM((tasks, blocks, chunk + piece, row_block), tiles.dtype),
            pltpu.SMEM(counts.shape, counts.dtype),
        ]
        + [pltpu.SemaphoreType.DMA((tasks,))] * 3
        + [pltpu.SemaphoreType.DMA],
        compiler_params=pltpu.CompilerParams(vmem_limit_bytes=58 << 20),
        name="pack",
    )(counts, tiles, pieces)


def pick_kernel(column, amplitudes, here, there, held, hot, picked, sems):
    row_tasks, slots, piece, _ = here.shape
    span = hot.shape[1]
    parts = sems.shape[1]
    core = lax.axis_index("core")

    def task_of(step):
        return 2 * lax.rem(step, row_tasks) + lax.rem(core + 1 + step // row_tasks, 2)

    def copy_of(step, part):
        rows = pl.ds(task_of(step) * piece + part * (piece // parts), piece // parts)
        return pltpu.make_async_copy(amplitudes.at[rows], held.at[rows], sems.at[step, part])

    for step in range(2 * row_tasks):
        for part in range(parts):
            copy_of(step, part).start()

    lane = lax.broadcasted_iota(jnp.int32, (1, span), 1)
    for n in range(slots):
        hot[pl.ds(n, 1), :] = jnp.where(lane == column[n], 1.0, 0.0)
    chosen = hot[...].astype(held.dtype)

    def one_task(step, out, row_task):
        for part in range(parts):
            copy_of(step, part).wait()
        base = task_of(step) * piece
        for c in range(piece):
            picked[c] = jnp.dot(chosen, held[base + c], preferred_element_type=jnp.float32)
        for n in range(slots):
            out[row_task, n] = picked[:, n, :].astype(out.dtype)

    @pl.loop(0, row_tasks)
    def _(step):
        one_task(step, there, step)

    @pl.loop(0, row_tasks)
    def _(step):
        one_task(row_tasks + step, here, step)


def pick(column, amplitudes, row_tasks):
    chunk, span, pair_total = amplitudes.shape
    slots = column.shape[0]
    piece = chunk // (2 * row_tasks)
    parts = 4
    part = jax.ShapeDtypeStruct((row_tasks, slots, piece, pair_total), amplitudes.dtype)
    in_vmem = pl.BlockSpec(memory_space=pltpu.VMEM)
    return pl.pallas_call(
        pick_kernel,
        out_shape=(part, part),
        in_specs=[pl.BlockSpec(memory_space=pltpu.SMEM), pl.BlockSpec(memory_space=pl.ANY)],
        out_specs=(in_vmem, in_vmem),
        scratch_shapes=[
            pltpu.VMEM(amplitudes.shape, amplitudes.dtype),
            pltpu.VMEM((slots, span), jnp.float32),
            pltpu.VMEM((piece, slots, pair_total), jnp.float32),
            pltpu.SemaphoreType.DMA((2 * row_tasks, parts)),
        ],
        compiler_params=pltpu.CompilerParams(vmem_limit_bytes=58 << 20),
        cost_estimate=pl.CostEstimate(
            flops=2 * slots * chunk * span * pair_total,
            bytes_accessed=2 * chunk * (span + slots) * pair_total,
            transcendentals=0,
        ),
        name="pick",
    )(column, amplitudes)


def ladder_kernel(meta, columns, here, other_core, other_row, tiles, keep, send, total, *, row_tasks, pair_blocks):
    mine = meta[2 * columns.shape[0] + 1]
    slots, _, chunk = columns.shape
    total[...] = jnp.zeros_like(total)

    def add_slots(step, carry):
        for part in range(4):
            n = step * 4 + part
            total[meta[n]] += jnp.dot(columns[n], tiles[n, :chunk], preferred_element_type=jnp.float32)
            second = here[mine, n] + other_core[mine, n] + other_row[n]
            total[meta[slots + n]] += lax.dot_general(
                second, tiles[n, chunk:], (((0,), (0,)), ((), ())), preferred_element_type=jnp.float32
            )
        return carry

    lax.fori_loop(0, slots // 4, add_slots, 0)

    core = meta[2 * slots]
    rows = NRB // (2 * row_tasks)
    pairs = total.shape[1] // pair_blocks
    for task in range(row_tasks):
        for block in range(pair_blocks):
            span = pl.ds(block * pairs, pairs)
            for row in range(rows):
                keep[block, task, row] = total[(2 * task + core) * rows + row, span, :]
                send[block, task, row] = total[(2 * task + 1 - core) * rows + row, span, :]


def body(amplitudes, integral_tiles, task_list, block_offsets, tile_counts, *, shape):
    blocks, row_tasks = shape
    tasks = 2 * row_tasks
    chunk, span, pair_total = amplitudes.shape
    row_block = integral_tiles.shape[5]
    slots = blocks * tasks
    piece = chunk // tasks
    rows, pairs = NRB // tasks, pair_total // blocks
    core = lax.axis_index("core").astype(jnp.int32)
    ty = lax.axis_index("ty").astype(jnp.int32)
    worker = ty * 2 + core

    sent = pack(integral_tiles, tile_counts, blocks).reshape(slots, chunk + piece, row_block)
    arrived = lax.all_to_all(sent, EVERY, 0, 0, tiled=True)

    lists = lax.all_gather(task_list * NRB + block_offsets, TASK, axis=1, tiled=True)
    counts, lists = lax.optimization_barrier((tile_counts, lists))
    busy = jnp.argmax(counts[:, 0], axis=-1).astype(jnp.int32)
    mine = lax.dynamic_index_in_dim(lists, worker, 2, keepdims=False)
    is_busy = busy[:, None, None] == jnp.arange(tasks, dtype=jnp.int32)
    second_row = jnp.sum(jnp.where(is_busy, lists[..., 1] % NRB, 0), axis=-1)
    meta = jnp.concatenate([(mine[..., 0] % NRB).reshape(-1), second_row.reshape(-1), core[None], ty[None]])

    virt = jnp.arange(span, dtype=jnp.int32)
    owner = (busy == worker)[:, None]
    column = jnp.where(owner, mine[..., 1] // NRB, span).reshape(-1)
    here, there = pick(column, amplitudes, row_tasks)
    other_core = lax.ppermute(there, "core", [(0, 1), (1, 0)])
    other_row = 0
    for hop in range(1, row_tasks):
        to = lax.rem(ty + hop, row_tasks)
        away = lax.dynamic_index_in_dim(here, to, 0, False) + lax.dynamic_index_in_dim(other_core, to, 0, False)
        other_row += lax.ppermute(away, "ty", [(i, (i + hop) % row_tasks) for i in range(row_tasks)])

    first = mine[..., 0] // NRB
    first, _ = lax.optimization_barrier((first, other_core))
    hot = first[..., None] == virt
    columns = jnp.einsum("nd,cdp->npc", hot.reshape(slots, span).astype(amplitudes.dtype), amplitudes)

    part = jax.ShapeDtypeStruct((blocks, row_tasks, rows, pairs, row_block), jnp.float32)
    in_vmem = pl.BlockSpec(memory_space=pltpu.VMEM)
    keep, send = pl.pallas_call(
        functools.partial(ladder_kernel, row_tasks=row_tasks, pair_blocks=blocks),
        out_shape=(part, part),
        in_specs=[pl.BlockSpec(memory_space=pltpu.SMEM)] + [in_vmem] * 5,
        out_specs=(in_vmem, in_vmem),
        scratch_shapes=[pltpu.VMEM((NRB, pair_total, row_block), jnp.float32)],
        compiler_params=pltpu.CompilerParams(vmem_limit_bytes=16 << 20),
        cost_estimate=pl.CostEstimate(
            flops=2 * slots * (chunk + piece) * pair_total * row_block,
            bytes_accessed=2 * slots * (chunk + piece) * (pair_total + row_block) + 4 * NRB * pair_total * row_block,
            transcendentals=0,
        ),
        name="ladder",
    )(meta, columns, here, other_core, other_row, arrived)

    other = lax.ppermute(send, "core", [(0, 1), (1, 0)])
    half = (keep + other).reshape(blocks * row_tasks, rows, pairs, row_block)
    parts = lax.all_to_all(half, ("blk", "ty"), 0, 0, tiled=True)
    out = jnp.sum(parts, axis=0)
    return jnp.transpose(out, (1, 0, 2)).reshape(pairs, rows * row_block)


def solution(mesh):
    blocks, tasks = mesh.shape["blk"], mesh.shape["task"]
    fine = Mesh(mesh.devices.reshape(blocks, tasks // 2, 2), EVERY)
    placed = (
        P("blk", TASK, None),
        P("blk", TASK, None, None, None, None),
        P(None, TASK, None, None),
        P(None, TASK, None, None),
        P(None, TASK, None),
    )
    return jax.shard_map(
        functools.partial(body, shape=(blocks, tasks // 2)),
        mesh=fine, in_specs=placed, out_specs=P("blk", TASK), check_vma=False,
    )
```

```python
import functools

import jax
import jax.numpy as jnp
from jax import lax
from jax.experimental import pallas as pl
from jax.experimental.pallas import tpu as pltpu
from jax.sharding import Mesh, PartitionSpec as P

NRB = 16
TASK = ("ty", "core")
EVERY = ("blk", "ty", "core")


def pack_kernel(counts, tiles, pieces, out, held, busy, first_sem, second_sem, out_sem, count_sem):
    tasks, blocks, rows, _ = held.shape
    chunk = tiles.shape[2]
    parts = first_sem.shape[1]
    count_copy = pltpu.make_async_copy(counts, busy, count_sem)
    count_copy.start()
    spans = [(w, part, pl.ds(part * (blocks // parts), blocks // parts)) for w in range(tasks) for part in range(parts)]
    first = [
        pltpu.make_async_copy(tiles.at[2 * w, span], held.at[w, span, pl.ds(0, chunk)], first_sem.at[w, part])
        for w, part, span in spans
    ]
    for copy in first:
        copy.start()
    count_copy.wait()
    group = lax.axis_index("blk")
    tile = 1
    for w in range(1, tasks):
        tile = jnp.where(busy[w, group] == 2, 2 * w + 1, tile)
    second = [
        pltpu.make_async_copy(
            pieces.at[tile, span, w], held.at[w, span, pl.ds(chunk, rows - chunk)], second_sem.at[w, part]
        )
        for w, part, span in spans
    ]
    for copy in second:
        copy.start()
    leave = [pltpu.make_async_copy(held.at[w, span], out.at[span, w], out_sem.at[w, part]) for w, part, span in spans]
    for n in range(len(spans)):
        first[n].wait()
        second[n].wait()
        leave[n].start()
    for copy in leave:
        copy.wait()


def pack(integral_tiles, tile_counts, blocks):
    tasks, _, virt_total, row_block = integral_tiles.shape[2:]
    chunk = virt_total // blocks
    piece = chunk // tasks
    tiles = integral_tiles.reshape(tasks * 2, blocks, chunk, row_block)
    pieces = integral_tiles.reshape(tasks * 2, blocks, tasks, piece, row_block)
    counts = jnp.transpose(tile_counts[:, 0])
    if piece % 16:
        own = lax.dynamic_index_in_dim(counts, lax.axis_index("blk"), 1, keepdims=False)
        second = lax.dynamic_index_in_dim(pieces, 2 * jnp.argmax(own) + 1, 0, keepdims=False)
        return jnp.concatenate([jnp.swapaxes(tiles[::2], 0, 1), second], axis=2)
    return pl.pallas_call(
        pack_kernel,
        out_shape=jax.ShapeDtypeStruct((blocks, tasks, chunk + piece, row_block), tiles.dtype),
        in_specs=[pl.BlockSpec(memory_space=pl.ANY)] * 3,
        out_specs=pl.BlockSpec(memory_space=pl.ANY),
        scratch_shapes=[
            pltpu.VMEM((tasks, blocks, chunk + piece, row_block), tiles.dtype),
            pltpu.SMEM(counts.shape, counts.dtype),
        ]
        + [pltpu.SemaphoreType.DMA((tasks, 4))] * 3
        + [pltpu.SemaphoreType.DMA],
        compiler_params=pltpu.CompilerParams(vmem_limit_bytes=58 << 20),
        name="pack",
    )(counts, tiles, pieces)


def pick_kernel(lists, amplitudes, there, here, *refs, hop, row_tasks):
    columns = refs[0] if len(refs) == 5 else None
    held, hot, picked, sems = refs[-4:]
    slots, piece, _ = here.shape
    sides, parts = sems.shape
    rows = piece // parts
    core, row_task = lax.axis_index("core"), lax.axis_index("ty") + hop

    def base_of(side):
        task = 2 * lax.rem(row_task + side // 2, row_tasks) + lax.rem(core + 1 + side, 2)
        return pl.multiple_of(task * piece, piece)

    def copy_of(side, part):
        return pltpu.make_async_copy(
            amplitudes.at[pl.ds(base_of(side) + part * rows, rows)],
            held.at[side, pl.ds(part * rows, rows)],
            sems.at[side, part],
        )

    for side in range(sides):
        for part in range(parts):
            copy_of(side, part).start()

    lane = lax.broadcasted_iota(jnp.int32, (1, hot.shape[1]), 1)
    for n in range(hot.shape[0]):
        hot[pl.ds(n, 1), :] = jnp.where(lane == lists[n], 1.0, 0.0)
    chosen = hot[...].astype(held.dtype)

    for side in range(sides):
        for part in range(parts):
            copy_of(side, part).wait()
            for c in range(part * rows, (part + 1) * rows):
                picked[c] = jnp.dot(chosen, held[side, c], preferred_element_type=jnp.float32)
        if side < 2:
            for n in range(slots):
                (there, here)[side][n] = picked[:, n, :].astype(here.dtype)
        if columns is not None:
            for n in range(slots):
                columns[n, pl.ds(base_of(side), piece), :] = picked[:, slots + n, :].astype(columns.dtype)


def pick(lists, amplitudes, hop, row_tasks, slots):
    chunk, span, pair_total = amplitudes.shape
    tasks = 2 * row_tasks
    piece = chunk // tasks
    listed = lists.shape[0]
    sides = tasks if listed > slots else 2
    part = jax.ShapeDtypeStruct((slots, piece, pair_total), amplitudes.dtype)
    whole = jax.ShapeDtypeStruct((slots, chunk, pair_total), amplitudes.dtype)
    outs = (part, part, whole) if listed > slots else (part, part)
    return pl.pallas_call(
        functools.partial(pick_kernel, hop=hop, row_tasks=row_tasks),
        out_shape=outs,
        in_specs=[pl.BlockSpec(memory_space=pltpu.SMEM), pl.BlockSpec(memory_space=pl.ANY)],
        out_specs=(pl.BlockSpec(memory_space=pltpu.VMEM),) * len(outs),
        scratch_shapes=[
            pltpu.VMEM((sides, piece, span, pair_total), amplitudes.dtype),
            pltpu.VMEM((listed, span), jnp.float32),
            pltpu.VMEM((piece, listed, pair_total), jnp.float32),
            pltpu.SemaphoreType.DMA((sides, 4)),
        ],
        compiler_params=pltpu.CompilerParams(vmem_limit_bytes=48 << 20),
        cost_estimate=pl.CostEstimate(
            flops=2 * listed * sides * piece * span * pair_total,
            bytes_accessed=2 * sides * piece * (span + listed) * pair_total,
            transcendentals=0,
        ),
        name="pick",
    )(lists, amplitudes)


def dot_rows(left, right):
    return lax.dot_general(left, right, (((0,), (0,)), ((), ())), preferred_element_type=jnp.float32)


def ladder_kernel(meta, columns, tiles, here, *refs, row_tasks, pair_blocks):
    others, (keep, send, total) = refs[:-3], refs[-3:]
    slots, chunk, _ = columns.shape
    total[...] = jnp.zeros_like(total)

    def add_slots(step, carry):
        for part in range(4):
            n = step * 4 + part
            total[meta[n]] += dot_rows(columns[n], tiles[n, :chunk])
            second = sum((other[n] for other in others), here[n])
            total[meta[slots + n]] += dot_rows(second, tiles[n, chunk:])
        return carry

    lax.fori_loop(0, slots // 4, add_slots, 0)

    core = meta[2 * slots]
    rows = NRB // (2 * row_tasks)
    pairs = total.shape[1] // pair_blocks
    for task in range(row_tasks):
        for block in range(pair_blocks):
            span = pl.ds(block * pairs, pairs)
            for row in range(rows):
                keep[block, task, row] = total[(2 * task + core) * rows + row, span, :]
                send[block, task, row] = total[(2 * task + 1 - core) * rows + row, span, :]


def body(amplitudes, integral_tiles, task_list, block_offsets, tile_counts, *, shape):
    blocks, row_tasks = shape
    tasks = 2 * row_tasks
    chunk, span, pair_total = amplitudes.shape
    row_block = integral_tiles.shape[5]
    slots = blocks * tasks
    piece = chunk // tasks
    rows, pairs = NRB // tasks, pair_total // blocks
    core = lax.axis_index("core").astype(jnp.int32)
    ty = lax.axis_index("ty").astype(jnp.int32)
    worker = ty * 2 + core

    sent = pack(integral_tiles, tile_counts, blocks).reshape(slots, chunk + piece, row_block)
    arrived = lax.all_to_all(sent, EVERY, 0, 0, tiled=True)

    lists = lax.all_gather(task_list * NRB + block_offsets, TASK, axis=1, tiled=True)
    counts, lists = lax.optimization_barrier((tile_counts[:, 0], lists))
    mine = lax.dynamic_index_in_dim(lists, worker, 2, keepdims=False)
    second_row = jnp.sum(jnp.where(counts[:, None] == 2, lists[..., 1] % NRB, 0), axis=-1)
    meta = jnp.concatenate([(mine[..., 0] % NRB).reshape(-1), second_row.reshape(-1), core[None]])

    owner = lax.dynamic_index_in_dim(counts, worker, 1) == 2
    column = jnp.where(owner, mine[..., 1] // NRB, span).reshape(-1)
    first = (mine[..., 0] // NRB).reshape(-1)
    others = []
    for hop in range(1, row_tasks):
        there, here = pick(column, amplitudes, hop, row_tasks, slots)
        away = here + lax.ppermute(there, "core", [(0, 1), (1, 0)])
        others.append(lax.ppermute(away, "ty", [(i, (i + hop) % row_tasks) for i in range(row_tasks)]))
        column, first, _ = lax.optimization_barrier((column, first, away))
    if piece % 16:
        there, here = pick(column, amplitudes, 0, row_tasks, slots)
        hot = (first[:, None] == jnp.arange(span, dtype=jnp.int32)).astype(amplitudes.dtype)
        columns = jnp.einsum("nd,cdp->ncp", hot, amplitudes)
    else:
        there, here, columns = pick(jnp.concatenate([column, first]), amplitudes, 0, row_tasks, slots)
    others.append(lax.ppermute(there, "core", [(0, 1), (1, 0)]))

    part = jax.ShapeDtypeStruct((blocks, row_tasks, rows, pairs, row_block), jnp.float32)
    in_vmem = pl.BlockSpec(memory_space=pltpu.VMEM)
    keep, send = pl.pallas_call(
        functools.partial(ladder_kernel, row_tasks=row_tasks, pair_blocks=blocks),
        out_shape=(part, part),
        in_specs=[pl.BlockSpec(memory_space=pltpu.SMEM)] + [in_vmem] * (3 + len(others)),
        out_specs=(in_vmem, in_vmem),
        scratch_shapes=[pltpu.VMEM((NRB, pair_total, row_block), jnp.float32)],
        compiler_params=pltpu.CompilerParams(vmem_limit_bytes=16 << 20),
        cost_estimate=pl.CostEstimate(
            flops=2 * slots * (chunk + piece) * pair_total * row_block,
            bytes_accessed=2 * slots * (chunk + piece) * (pair_total + row_block) + 4 * NRB * pair_total * row_block,
            transcendentals=0,
        ),
        name="ladder",
    )(meta, columns, arrived, here, *others)

    other = lax.ppermute(send, "core", [(0, 1), (1, 0)])
    half = (keep + other).reshape(blocks * row_tasks, rows, pairs, row_block)
    parts = lax.all_to_all(half, ("blk", "ty"), 0, 0, tiled=True)
    out = jnp.sum(parts, axis=0)
    return jnp.transpose(out, (1, 0, 2)).reshape(pairs, rows * row_block)


def solution(mesh):
    blocks, tasks = mesh.shape["blk"], mesh.shape["task"]
    fine = Mesh(mesh.devices.reshape(blocks, tasks // 2, 2), EVERY)
    placed = (
        P("blk", TASK, None),
        P("blk", TASK, None, None, None, None),
        P(None, TASK, None, None),
        P(None, TASK, None, None),
        P(None, TASK, None),
    )
    return jax.shard_map(
        functools.partial(body, shape=(blocks, tasks // 2)),
        mesh=fine, in_specs=placed, out_specs=P("blk", TASK), check_vma=False,
    )
```

```python
import functools

import jax
import jax.numpy as jnp
from jax import lax
from jax.experimental import pallas as pl
from jax.experimental.pallas import tpu as pltpu
from jax.sharding import Mesh, PartitionSpec as P

NRB = 16
TASK = ("ty", "core")
EVERY = ("blk", "ty", "core")


def pack_kernel(counts, tiles, pieces, out, held, busy, in_sem, out_sem, count_sem):
    tasks, _, rows, _ = held.shape
    chunk = tiles.shape[2]
    upper, lower = pl.ds(0, chunk), pl.ds(chunk, rows - chunk)
    count_copy = pltpu.make_async_copy(counts, busy, count_sem)
    count_copy.start()
    first = [pltpu.make_async_copy(tiles.at[2 * w], held.at[w, :, upper], in_sem.at[0, w]) for w in range(tasks)]
    for copy in first:
        copy.start()
    count_copy.wait()
    group = lax.axis_index("blk")
    tile = 1
    for w in range(1, tasks):
        tile = jnp.where(busy[w, group] == 2, 2 * w + 1, tile)
    second = [
        pltpu.make_async_copy(pieces.at[tile, :, w], held.at[w, :, lower], in_sem.at[1, w]) for w in range(tasks)
    ]
    for copy in second:
        copy.start()
    leave = [
        pltpu.make_async_copy(held.at[w, :, span], out.at[:, w, span], out_sem.at[half, w])
        for half, span in enumerate((upper, lower))
        for w in range(tasks)
    ]
    for arrive, go in zip(first + second, leave):
        arrive.wait()
        go.start()
    for copy in leave:
        copy.wait()


def pack(integral_tiles, tile_counts, blocks):
    tasks, _, virt_total, row_block = integral_tiles.shape[2:]
    chunk = virt_total // blocks
    piece = chunk // tasks
    tiles = integral_tiles.reshape(tasks * 2, blocks, chunk, row_block)
    pieces = integral_tiles.reshape(tasks * 2, blocks, tasks, piece, row_block)
    counts = jnp.transpose(tile_counts[:, 0])
    if piece % 16:
        own = lax.dynamic_index_in_dim(counts, lax.axis_index("blk"), 1, keepdims=False)
        second = lax.dynamic_index_in_dim(pieces, 2 * jnp.argmax(own) + 1, 0, keepdims=False)
        return jnp.concatenate([jnp.swapaxes(tiles[::2], 0, 1), second], axis=2)
    return pl.pallas_call(
        pack_kernel,
        out_shape=jax.ShapeDtypeStruct((blocks, tasks, chunk + piece, row_block), tiles.dtype),
        in_specs=[pl.BlockSpec(memory_space=pl.ANY)] * 3,
        out_specs=pl.BlockSpec(memory_space=pl.ANY),
        scratch_shapes=[
            pltpu.VMEM((tasks, blocks, chunk + piece, row_block), tiles.dtype),
            pltpu.SMEM(counts.shape, counts.dtype),
        ]
        + [pltpu.SemaphoreType.DMA((2, tasks))] * 2
        + [pltpu.SemaphoreType.DMA],
        compiler_params=pltpu.CompilerParams(vmem_limit_bytes=58 << 20),
        name="pack",
    )(counts, tiles, pieces)


def pick_kernel(lists, amplitudes, there, here, *refs, hop, row_tasks):
    columns = refs[0] if len(refs) == 5 else None
    held, hot, picked, sems = refs[-4:]
    slots, piece, _ = here.shape
    sides, parts = sems.shape
    rows = piece // parts
    core, row_task = lax.axis_index("core"), lax.axis_index("ty") + hop

    def base_of(side):
        task = 2 * lax.rem(row_task + side // 2, row_tasks) + lax.rem(core + 1 + side, 2)
        return pl.multiple_of(task * piece, piece)

    def copy_of(side, part):
        return pltpu.make_async_copy(
            amplitudes.at[pl.ds(base_of(side) + part * rows, rows)],
            held.at[side, pl.ds(part * rows, rows)],
            sems.at[side, part],
        )

    for side in range(sides):
        for part in range(parts):
            copy_of(side, part).start()

    lane = lax.broadcasted_iota(jnp.int32, (1, hot.shape[1]), 1)
    for n in range(hot.shape[0]):
        hot[pl.ds(n, 1), :] = jnp.where(lane == lists[n], 1.0, 0.0)
    chosen = hot[...].astype(held.dtype)

    for side in range(sides):
        for part in range(parts):
            copy_of(side, part).wait()
            for c in range(part * rows, (part + 1) * rows):
                picked[c] = jnp.dot(chosen, held[side, c], preferred_element_type=jnp.float32)
        if side < 2:
            for n in range(slots):
                (there, here)[side][n] = picked[:, n, :].astype(here.dtype)
        if columns is not None:
            for n in range(slots):
                columns[n, pl.ds(base_of(side), piece), :] = picked[:, slots + n, :].astype(columns.dtype)


def pick(lists, amplitudes, hop, row_tasks, slots):
    chunk, span, pair_total = amplitudes.shape
    tasks = 2 * row_tasks
    piece = chunk // tasks
    listed = lists.shape[0]
    sides = tasks if listed > slots else 2
    part = jax.ShapeDtypeStruct((slots, piece, pair_total), amplitudes.dtype)
    whole = jax.ShapeDtypeStruct((slots, chunk, pair_total), amplitudes.dtype)
    outs = (part, part, whole) if listed > slots else (part, part)
    return pl.pallas_call(
        functools.partial(pick_kernel, hop=hop, row_tasks=row_tasks),
        out_shape=outs,
        in_specs=[pl.BlockSpec(memory_space=pltpu.SMEM), pl.BlockSpec(memory_space=pl.ANY)],
        out_specs=(pl.BlockSpec(memory_space=pltpu.VMEM),) * len(outs),
        scratch_shapes=[
            pltpu.VMEM((sides, piece, span, pair_total), amplitudes.dtype),
            pltpu.VMEM((listed, span), jnp.float32),
            pltpu.VMEM((piece, listed, pair_total), jnp.float32),
            pltpu.SemaphoreType.DMA((sides, 4)),
        ],
        compiler_params=pltpu.CompilerParams(vmem_limit_bytes=48 << 20),
        cost_estimate=pl.CostEstimate(
            flops=2 * listed * sides * piece * span * pair_total,
            bytes_accessed=2 * sides * piece * (span + listed) * pair_total,
            transcendentals=0,
        ),
        name="pick",
    )(lists, amplitudes)


def dot_rows(left, right):
    return lax.dot_general(left, right, (((0,), (0,)), ((), ())), preferred_element_type=jnp.float32)


def ladder_kernel(meta, columns, tiles, extras, keep, send, total, *, row_tasks, pair_blocks):
    slots, chunk, _ = columns.shape
    total[...] = jnp.zeros_like(total)

    group = min(slots, 32)

    def add_slots(step, carry):
        for part in range(group):
            n = step * group + part
            total[meta[n]] += dot_rows(columns[n], tiles[n, :chunk])
            total[meta[slots + n]] += dot_rows(extras[n], tiles[n, chunk:])
        return carry

    lax.fori_loop(0, slots // group, add_slots, 0)

    core = meta[2 * slots]
    rows = NRB // (2 * row_tasks)
    pairs = total.shape[1] // pair_blocks
    for task in range(row_tasks):
        for block in range(pair_blocks):
            span = pl.ds(block * pairs, pairs)
            for row in range(rows):
                keep[block, task, row] = total[(2 * task + core) * rows + row, span, :]
                send[block, task, row] = total[(2 * task + 1 - core) * rows + row, span, :]


def body(amplitudes, integral_tiles, task_list, block_offsets, tile_counts, *, shape):
    blocks, row_tasks = shape
    tasks = 2 * row_tasks
    chunk, span, pair_total = amplitudes.shape
    row_block = integral_tiles.shape[5]
    slots = blocks * tasks
    piece = chunk // tasks
    rows, pairs = NRB // tasks, pair_total // blocks
    core = lax.axis_index("core").astype(jnp.int32)
    ty = lax.axis_index("ty").astype(jnp.int32)
    worker = ty * 2 + core

    sent = pack(integral_tiles, tile_counts, blocks).reshape(slots, chunk + piece, row_block)
    arrived = lax.all_to_all(sent, EVERY, 0, 0, tiled=True)

    lists = lax.all_gather(task_list * NRB + block_offsets, TASK, axis=1, tiled=True)
    counts, lists = lax.optimization_barrier((tile_counts[:, 0], lists))
    mine = lax.dynamic_index_in_dim(lists, worker, 2, keepdims=False)
    second_row = jnp.sum(jnp.where(counts[:, None] == 2, lists[..., 1] % NRB, 0), axis=-1)
    meta = jnp.concatenate([(mine[..., 0] % NRB).reshape(-1), second_row.reshape(-1), core[None]])

    owner = lax.dynamic_index_in_dim(counts, worker, 1) == 2
    column = jnp.where(owner, mine[..., 1] // NRB, span).reshape(-1)
    first = (mine[..., 0] // NRB).reshape(-1)
    others = []
    for hop in range(1, row_tasks):
        there, here = pick(column, amplitudes, hop, row_tasks, slots)
        away = here + lax.ppermute(there, "core", [(0, 1), (1, 0)])
        others.append(lax.ppermute(away, "ty", [(i, (i + hop) % row_tasks) for i in range(row_tasks)]))
        column, first, _ = lax.optimization_barrier((column, first, away))
    if piece % 16:
        there, here = pick(column, amplitudes, 0, row_tasks, slots)
        hot = (first[:, None] == jnp.arange(span, dtype=jnp.int32)).astype(amplitudes.dtype)
        columns = jnp.einsum("nd,cdp->ncp", hot, amplitudes)
    else:
        there, here, columns = pick(jnp.concatenate([column, first]), amplitudes, 0, row_tasks, slots)
    others.append(lax.ppermute(there, "core", [(0, 1), (1, 0)]))
    extras = sum(others, here)

    part = jax.ShapeDtypeStruct((blocks, row_tasks, rows, pairs, row_block), jnp.float32)
    in_vmem = pl.BlockSpec(memory_space=pltpu.VMEM)
    keep, send = pl.pallas_call(
        functools.partial(ladder_kernel, row_tasks=row_tasks, pair_blocks=blocks),
        out_shape=(part, part),
        in_specs=[pl.BlockSpec(memory_space=pltpu.SMEM)] + [in_vmem] * 3,
        out_specs=(in_vmem, in_vmem),
        scratch_shapes=[pltpu.VMEM((NRB, pair_total, row_block), jnp.float32)],
        compiler_params=pltpu.CompilerParams(vmem_limit_bytes=16 << 20),
        cost_estimate=pl.CostEstimate(
            flops=2 * slots * (chunk + piece) * pair_total * row_block,
            bytes_accessed=2 * slots * (chunk + piece) * (pair_total + row_block) + 4 * NRB * pair_total * row_block,
            transcendentals=0,
        ),
        name="ladder",
    )(meta, columns, arrived, extras)

    other = lax.ppermute(send, "core", [(0, 1), (1, 0)])
    half = (keep + other).reshape(blocks * row_tasks, rows, pairs, row_block)
    parts = lax.all_to_all(half, ("blk", "ty"), 0, 0, tiled=True)
    out = jnp.sum(parts, axis=0)
    return jnp.transpose(out, (1, 0, 2)).reshape(pairs, rows * row_block)


def solution(mesh):
    blocks, tasks = mesh.shape["blk"], mesh.shape["task"]
    fine = Mesh(mesh.devices.reshape(blocks, tasks // 2, 2), EVERY)
    placed = (
        P("blk", TASK, None),
        P("blk", TASK, None, None, None, None),
        P(None, TASK, None, None),
        P(None, TASK, None, None),
        P(None, TASK, None),
    )
    return jax.shard_map(
        functools.partial(body, shape=(blocks, tasks // 2)),
        mesh=fine, in_specs=placed, out_specs=P("blk", TASK), check_vma=False,
    )
```

```python
import functools

import jax
import jax.numpy as jnp
from jax import lax
from jax.experimental import pallas as pl
from jax.experimental.pallas import tpu as pltpu
from jax.sharding import Mesh, PartitionSpec as P

NRB = 16
TASK = ("ty", "core")
EVERY = ("blk", "ty", "core")


def pack_kernel(counts, tiles, pieces, out, held, busy, in_sem, out_sem, count_sem):
    tasks, _, rows, _ = held.shape
    chunk = tiles.shape[2]
    upper, lower = pl.ds(0, chunk), pl.ds(chunk, rows - chunk)
    count_copy = pltpu.make_async_copy(counts, busy, count_sem)
    count_copy.start()
    first = [pltpu.make_async_copy(tiles.at[2 * w], held.at[w, :, upper], in_sem.at[0, w]) for w in range(tasks)]
    for copy in first:
        copy.start()
    count_copy.wait()
    group = lax.axis_index("blk")
    tile = 1
    for w in range(1, tasks):
        tile = jnp.where(busy[w, group] == 2, 2 * w + 1, tile)
    second = [
        pltpu.make_async_copy(pieces.at[tile, :, w], held.at[w, :, lower], in_sem.at[1, w]) for w in range(tasks)
    ]
    for copy in second:
        copy.start()
    leave = [
        pltpu.make_async_copy(held.at[w, :, span], out.at[:, w, span], out_sem.at[half, w])
        for half, span in enumerate((upper, lower))
        for w in range(tasks)
    ]
    for arrive, go in zip(first + second, leave):
        arrive.wait()
        go.start()
    for copy in leave:
        copy.wait()


def pack(integral_tiles, tile_counts, blocks):
    tasks, _, virt_total, row_block = integral_tiles.shape[2:]
    chunk = virt_total // blocks
    piece = chunk // tasks
    tiles = integral_tiles.reshape(tasks * 2, blocks, chunk, row_block)
    pieces = integral_tiles.reshape(tasks * 2, blocks, tasks, piece, row_block)
    counts = jnp.transpose(tile_counts[:, 0])
    if piece % 16:
        own = lax.dynamic_index_in_dim(counts, lax.axis_index("blk"), 1, keepdims=False)
        second = lax.dynamic_index_in_dim(pieces, 2 * jnp.argmax(own) + 1, 0, keepdims=False)
        return jnp.concatenate([jnp.swapaxes(tiles[::2], 0, 1), second], axis=2)
    return pl.pallas_call(
        pack_kernel,
        out_shape=jax.ShapeDtypeStruct((blocks, tasks, chunk + piece, row_block), tiles.dtype),
        in_specs=[pl.BlockSpec(memory_space=pl.ANY)] * 3,
        out_specs=pl.BlockSpec(memory_space=pl.ANY),
        scratch_shapes=[
            pltpu.VMEM((tasks, blocks, chunk + piece, row_block), tiles.dtype),
            pltpu.SMEM(counts.shape, counts.dtype),
        ]
        + [pltpu.SemaphoreType.DMA((2, tasks))] * 2
        + [pltpu.SemaphoreType.DMA],
        compiler_params=pltpu.CompilerParams(vmem_limit_bytes=58 << 20),
        name="pack",
    )(counts, tiles, pieces)


def pick_kernel(lists, amplitudes, there, here, *refs, hop, row_tasks):
    columns = refs[0] if len(refs) == 5 else None
    held, hot, picked, sems = refs[-4:]
    slots, piece, _ = here.shape
    sides, parts = sems.shape
    rows = piece // parts
    core, row_task = lax.axis_index("core"), lax.axis_index("ty") + hop

    def base_of(side):
        task = 2 * lax.rem(row_task + side // 2, row_tasks) + lax.rem(core + 1 + side, 2)
        return pl.multiple_of(task * piece, piece)

    def copy_of(side, part):
        return pltpu.make_async_copy(
            amplitudes.at[pl.ds(base_of(side) + part * rows, rows)],
            held.at[side, pl.ds(part * rows, rows)],
            sems.at[side, part],
        )

    for side in range(sides):
        for part in range(parts):
            copy_of(side, part).start()

    lane = lax.broadcasted_iota(jnp.int32, (1, hot.shape[1]), 1)
    for n in range(hot.shape[0]):
        hot[pl.ds(n, 1), :] = jnp.where(lane == lists[n], 1.0, 0.0)
    chosen = hot[...].astype(held.dtype)

    for side in range(sides):
        for part in range(parts):
            copy_of(side, part).wait()
            for c in range(part * rows, (part + 1) * rows):
                picked[c] = jnp.dot(chosen, held[side, c], preferred_element_type=jnp.float32)
        if side < 2:
            for n in range(slots):
                (there, here)[side][n] = picked[:, n, :].astype(here.dtype)
        if columns is not None:
            for n in range(slots):
                columns[n, pl.ds(base_of(side), piece), :] = picked[:, slots + n, :].astype(columns.dtype)


def pick(lists, amplitudes, hop, row_tasks, slots):
    chunk, span, pair_total = amplitudes.shape
    tasks = 2 * row_tasks
    piece = chunk // tasks
    listed = lists.shape[0]
    sides = tasks if listed > slots else 2
    part = jax.ShapeDtypeStruct((slots, piece, pair_total), amplitudes.dtype)
    whole = jax.ShapeDtypeStruct((slots, chunk, pair_total), amplitudes.dtype)
    outs = (part, part, whole) if listed > slots else (part, part)
    return pl.pallas_call(
        functools.partial(pick_kernel, hop=hop, row_tasks=row_tasks),
        out_shape=outs,
        in_specs=[pl.BlockSpec(memory_space=pltpu.SMEM), pl.BlockSpec(memory_space=pl.ANY)],
        out_specs=(pl.BlockSpec(memory_space=pltpu.VMEM),) * len(outs),
        scratch_shapes=[
            pltpu.VMEM((sides, piece, span, pair_total), amplitudes.dtype),
            pltpu.VMEM((listed, span), jnp.float32),
            pltpu.VMEM((piece, listed, pair_total), jnp.float32),
            pltpu.SemaphoreType.DMA((sides, 4)),
        ],
        compiler_params=pltpu.CompilerParams(vmem_limit_bytes=48 << 20),
        cost_estimate=pl.CostEstimate(
            flops=2 * listed * sides * piece * span * pair_total,
            bytes_accessed=2 * sides * piece * (span + listed) * pair_total,
            transcendentals=0,
        ),
        name="pick",
    )(lists, amplitudes)


def dot_rows(left, right):
    return lax.dot_general(left, right, (((0,), (0,)), ((), ())), preferred_element_type=jnp.float32)


def ladder_kernel(meta, columns, tiles, extras, keep, send, total, *, row_tasks, pair_blocks):
    slots, chunk, _ = columns.shape
    total[...] = jnp.zeros_like(total)

    group = min(slots, 32)

    def add_slots(step, carry):
        for part in range(group):
            n = step * group + part
            total[meta[n]] += dot_rows(columns[n], tiles[n, :chunk])
            total[meta[slots + n]] += dot_rows(extras[n], tiles[n, chunk:])
        return carry

    lax.fori_loop(0, slots // group, add_slots, 0)

    core = meta[2 * slots]
    rows = NRB // (2 * row_tasks)
    pairs = total.shape[1] // pair_blocks
    for task in range(row_tasks):
        for block in range(pair_blocks):
            span = pl.ds(block * pairs, pairs)
            for row in range(rows):
                keep[block, task, row] = total[(2 * task + core) * rows + row, span, :]
                send[block, task, row] = total[(2 * task + 1 - core) * rows + row, span, :]


STEPS, TOP, FLOOR = 64.0, 32752.0, 2.0**-111


def code_kernel(keep, other, out):
    rows = out.shape[1] - 8
    lane = lax.broadcasted_iota(jnp.int32, (8, out.shape[2]), 1)
    for to in range(out.shape[0]):
        value = (keep[to] + other[to]).reshape(rows, out.shape[2])
        largest = jnp.maximum(jnp.max(jnp.abs(value), axis=1, keepdims=True), FLOOR)
        level = jnp.floor(jnp.log2(largest) * STEPS) + 2.0
        out[to, :rows] = jnp.round(value * (jnp.exp2(level * (-1.0 / STEPS)) * TOP)).astype(jnp.int32).astype(jnp.int16)
        scales = jnp.zeros(lane.shape, jnp.float32)
        for group in range(rows // 8):
            scales = jnp.where(lane == group, level[8 * group : 8 * group + 8], scales)
        out[to, rows:] = scales.astype(jnp.int32).astype(jnp.int16)


def decode_kernel(parts, out):
    pairs, width = out.shape[0], parts.shape[2]
    rows = parts.shape[1] - 8
    total = [jnp.zeros((8, width), jnp.float32)] * (rows // 8)
    for source in range(parts.shape[0]):
        scales = jnp.exp2(parts[source, rows:].astype(jnp.int32).astype(jnp.float32) * (1.0 / STEPS)) * (1.0 / TOP)
        value = parts[source, :rows].astype(jnp.int32).astype(jnp.float32)
        for group in range(rows // 8):
            total[group] += value[8 * group : 8 * group + 8] * scales[:, group : group + 1]
    for group in range(rows // 8):
        first = 8 * group
        out[first % pairs : first % pairs + 8, first // pairs * width : (first // pairs + 1) * width] = total[group]


def body(amplitudes, integral_tiles, task_list, block_offsets, tile_counts, *, shape):
    blocks, row_tasks = shape
    tasks = 2 * row_tasks
    chunk, span, pair_total = amplitudes.shape
    row_block = integral_tiles.shape[5]
    slots = blocks * tasks
    piece = chunk // tasks
    rows, pairs = NRB // tasks, pair_total // blocks
    core = lax.axis_index("core").astype(jnp.int32)
    ty = lax.axis_index("ty").astype(jnp.int32)
    worker = ty * 2 + core

    sent = pack(integral_tiles, tile_counts, blocks).reshape(slots, chunk + piece, row_block)
    arrived = lax.all_to_all(sent, EVERY, 0, 0, tiled=True)

    lists = lax.all_gather(task_list * NRB + block_offsets, TASK, axis=1, tiled=True)
    counts, lists = lax.optimization_barrier((tile_counts[:, 0], lists))
    mine = lax.dynamic_index_in_dim(lists, worker, 2, keepdims=False)
    second_row = jnp.sum(jnp.where(counts[:, None] == 2, lists[..., 1] % NRB, 0), axis=-1)
    meta = jnp.concatenate([(mine[..., 0] % NRB).reshape(-1), second_row.reshape(-1), core[None]])

    owner = lax.dynamic_index_in_dim(counts, worker, 1) == 2
    column = jnp.where(owner, mine[..., 1] // NRB, span).reshape(-1)
    first = (mine[..., 0] // NRB).reshape(-1)
    others = []
    for hop in range(1, row_tasks):
        there, here = pick(column, amplitudes, hop, row_tasks, slots)
        away = here + lax.ppermute(there, "core", [(0, 1), (1, 0)])
        others.append(lax.ppermute(away, "ty", [(i, (i + hop) % row_tasks) for i in range(row_tasks)]))
        column, first, _ = lax.optimization_barrier((column, first, away))
    if piece % 16:
        there, here = pick(column, amplitudes, 0, row_tasks, slots)
        hot = (first[:, None] == jnp.arange(span, dtype=jnp.int32)).astype(amplitudes.dtype)
        columns = jnp.einsum("nd,cdp->ncp", hot, amplitudes)
    else:
        there, here, columns = pick(jnp.concatenate([column, first]), amplitudes, 0, row_tasks, slots)
    others.append(lax.ppermute(there, "core", [(0, 1), (1, 0)]))
    extras = sum(others, here)

    part = jax.ShapeDtypeStruct((blocks, row_tasks, rows, pairs, row_block), jnp.float32)
    in_vmem = pl.BlockSpec(memory_space=pltpu.VMEM)
    keep, send = pl.pallas_call(
        functools.partial(ladder_kernel, row_tasks=row_tasks, pair_blocks=blocks),
        out_shape=(part, part),
        in_specs=[pl.BlockSpec(memory_space=pltpu.SMEM)] + [in_vmem] * 3,
        out_specs=(in_vmem, in_vmem),
        scratch_shapes=[pltpu.VMEM((NRB, pair_total, row_block), jnp.float32)],
        compiler_params=pltpu.CompilerParams(vmem_limit_bytes=16 << 20),
        cost_estimate=pl.CostEstimate(
            flops=2 * slots * (chunk + piece) * pair_total * row_block,
            bytes_accessed=2 * slots * (chunk + piece) * (pair_total + row_block) + 4 * NRB * pair_total * row_block,
            transcendentals=0,
        ),
        name="ladder",
    )(meta, columns, arrived, extras)

    other = lax.ppermute(send, "core", [(0, 1), (1, 0)])
    peers = blocks * row_tasks
    cut = (peers, rows, pairs, row_block)
    coded = pl.pallas_call(
        code_kernel,
        out_shape=jax.ShapeDtypeStruct((peers, rows * pairs + 8, row_block), jnp.int16),
        in_specs=[in_vmem, in_vmem],
        out_specs=in_vmem,
        compiler_params=pltpu.CompilerParams(vmem_limit_bytes=16 << 20),
        name="code",
    )(keep.reshape(cut), other.reshape(cut))
    parts = lax.all_to_all(coded, ("blk", "ty"), 0, 0, tiled=True)
    return pl.pallas_call(
        decode_kernel,
        out_shape=jax.ShapeDtypeStruct((pairs, rows * row_block), jnp.float32),
        in_specs=[in_vmem],
        out_specs=in_vmem,
        compiler_params=pltpu.CompilerParams(vmem_limit_bytes=16 << 20),
        name="decode",
    )(parts)


def solution(mesh):
    blocks, tasks = mesh.shape["blk"], mesh.shape["task"]
    fine = Mesh(mesh.devices.reshape(blocks, tasks // 2, 2), EVERY)
    placed = (
        P("blk", TASK, None),
        P("blk", TASK, None, None, None, None),
        P(None, TASK, None, None),
        P(None, TASK, None, None),
        P(None, TASK, None),
    )
    return jax.shard_map(
        functools.partial(body, shape=(blocks, tasks // 2)),
        mesh=fine, in_specs=placed, out_specs=P("blk", TASK), check_vma=False,
    )
```

```python
import functools

import jax
import jax.numpy as jnp
from jax import lax
from jax.experimental import pallas as pl
from jax.experimental.pallas import tpu as pltpu
from jax.sharding import Mesh, PartitionSpec as P

NRB = 16
TASK = ("ty", "core")
EVERY = ("blk", "ty", "core")


def pack_kernel(counts, tiles, pieces, out, held, busy, in_sem, out_sem, count_sem):
    tasks, _, rows, _ = held.shape
    chunk = tiles.shape[2]
    upper, lower = pl.ds(0, chunk), pl.ds(chunk, rows - chunk)
    count_copy = pltpu.make_async_copy(counts, busy, count_sem)
    count_copy.start()
    first = [pltpu.make_async_copy(tiles.at[2 * w], held.at[w, :, upper], in_sem.at[0, w]) for w in range(tasks)]
    for copy in first:
        copy.start()
    count_copy.wait()
    group = lax.axis_index("blk")
    tile = 1
    for w in range(1, tasks):
        tile = jnp.where(busy[w, group] == 2, 2 * w + 1, tile)
    second = [
        pltpu.make_async_copy(pieces.at[tile, :, w], held.at[w, :, lower], in_sem.at[1, w]) for w in range(tasks)
    ]
    for copy in second:
        copy.start()
    leave = [
        pltpu.make_async_copy(held.at[w, :, span], out.at[:, w, span], out_sem.at[half, w])
        for half, span in enumerate((upper, lower))
        for w in range(tasks)
    ]
    for arrive, go in zip(first + second, leave):
        arrive.wait()
        go.start()
    for copy in leave:
        copy.wait()


def pack(integral_tiles, tile_counts, blocks):
    tasks, _, virt_total, row_block = integral_tiles.shape[2:]
    chunk = virt_total // blocks
    piece = chunk // tasks
    tiles = integral_tiles.reshape(tasks * 2, blocks, chunk, row_block)
    pieces = integral_tiles.reshape(tasks * 2, blocks, tasks, piece, row_block)
    counts = jnp.transpose(tile_counts[:, 0])
    if piece % 16:
        own = lax.dynamic_index_in_dim(counts, lax.axis_index("blk"), 1, keepdims=False)
        second = lax.dynamic_index_in_dim(pieces, 2 * jnp.argmax(own) + 1, 0, keepdims=False)
        return jnp.concatenate([jnp.swapaxes(tiles[::2], 0, 1), second], axis=2)
    return pl.pallas_call(
        pack_kernel,
        out_shape=jax.ShapeDtypeStruct((blocks, tasks, chunk + piece, row_block), tiles.dtype),
        in_specs=[pl.BlockSpec(memory_space=pl.ANY)] * 3,
        out_specs=pl.BlockSpec(memory_space=pl.ANY),
        scratch_shapes=[
            pltpu.VMEM((tasks, blocks, chunk + piece, row_block), tiles.dtype),
            pltpu.SMEM(counts.shape, counts.dtype),
        ]
        + [pltpu.SemaphoreType.DMA((2, tasks))] * 2
        + [pltpu.SemaphoreType.DMA],
        compiler_params=pltpu.CompilerParams(vmem_limit_bytes=58 << 20),
        name="pack",
    )(counts, tiles, pieces)


def pick_kernel(lists, amplitudes, there, here, *refs, hop, row_tasks):
    columns = refs[0] if len(refs) == 5 else None
    held, hot, picked, sems = refs[-4:]
    slots, piece, _ = here.shape
    sides, parts = sems.shape
    rows = piece // parts
    core, row_task = lax.axis_index("core"), lax.axis_index("ty") + hop

    def base_of(side):
        task = 2 * lax.rem(row_task + side // 2, row_tasks) + lax.rem(core + 1 + side, 2)
        return pl.multiple_of(task * piece, piece)

    def copy_of(side, part):
        return pltpu.make_async_copy(
            amplitudes.at[pl.ds(base_of(side) + part * rows, rows)],
            held.at[side, pl.ds(part * rows, rows)],
            sems.at[side, part],
        )

    for side in range(sides):
        for part in range(parts):
            copy_of(side, part).start()

    lane = lax.broadcasted_iota(jnp.int32, (1, hot.shape[1]), 1)
    for n in range(hot.shape[0]):
        hot[pl.ds(n, 1), :] = jnp.where(lane == lists[n], 1.0, 0.0)
    chosen = hot[...].astype(held.dtype)

    for side in range(sides):
        for part in range(parts):
            copy_of(side, part).wait()
            for c in range(part * rows, (part + 1) * rows):
                picked[c] = jnp.dot(chosen, held[side, c], preferred_element_type=jnp.float32)
        if side < 2:
            for n in range(slots):
                (there, here)[side][n] = picked[:, n, :].astype(here.dtype)
        if columns is not None:
            for n in range(slots):
                columns[n, pl.ds(base_of(side), piece), :] = picked[:, slots + n, :].astype(columns.dtype)


def pick(lists, amplitudes, hop, row_tasks, slots):
    chunk, span, pair_total = amplitudes.shape
    tasks = 2 * row_tasks
    piece = chunk // tasks
    listed = lists.shape[0]
    sides = tasks if listed > slots else 2
    part = jax.ShapeDtypeStruct((slots, piece, pair_total), amplitudes.dtype)
    whole = jax.ShapeDtypeStruct((slots, chunk, pair_total), amplitudes.dtype)
    outs = (part, part, whole) if listed > slots else (part, part)
    return pl.pallas_call(
        functools.partial(pick_kernel, hop=hop, row_tasks=row_tasks),
        out_shape=outs,
        in_specs=[pl.BlockSpec(memory_space=pltpu.SMEM), pl.BlockSpec(memory_space=pl.ANY)],
        out_specs=(pl.BlockSpec(memory_space=pltpu.VMEM),) * len(outs),
        scratch_shapes=[
            pltpu.VMEM((sides, piece, span, pair_total), amplitudes.dtype),
            pltpu.VMEM((listed, span), jnp.float32),
            pltpu.VMEM((piece, listed, pair_total), jnp.float32),
            pltpu.SemaphoreType.DMA((sides, 4)),
        ],
        compiler_params=pltpu.CompilerParams(vmem_limit_bytes=48 << 20),
        cost_estimate=pl.CostEstimate(
            flops=2 * listed * sides * piece * span * pair_total,
            bytes_accessed=2 * sides * piece * (span + listed) * pair_total,
            transcendentals=0,
        ),
        name="pick",
    )(lists, amplitudes)


def dot_rows(left, right):
    return lax.dot_general(left, right, (((0,), (0,)), ((), ())), preferred_element_type=jnp.float32)


def ladder_kernel(meta, columns, tiles, extras, send, total, *, row_tasks, pair_blocks):
    slots, chunk, _ = columns.shape
    total[...] = jnp.zeros_like(total)

    group = min(slots, 32)

    def add_slots(step, carry):
        for part in range(group):
            n = step * group + part
            total[meta[n]] += dot_rows(columns[n], tiles[n, :chunk])
            total[meta[slots + n]] += dot_rows(extras[n], tiles[n, chunk:])
        return carry

    lax.fori_loop(0, slots // group, add_slots, 0)

    core = meta[2 * slots]
    rows = NRB // (2 * row_tasks)
    pairs = total.shape[1] // pair_blocks
    for task in range(row_tasks):
        for block in range(pair_blocks):
            span = pl.ds(block * pairs, pairs)
            for row in range(rows):
                send[block, task, row] = total[(2 * task + 1 - core) * rows + row, span, :]


STEPS, TOP, FLOOR = 64.0, 32752.0, 2.0**-111


def code_kernel(total, other, out, *, row_tasks):
    peers, blocks, pairs, width = other.shape
    rows = blocks * pairs
    core = lax.axis_index("core")
    lane = lax.broadcasted_iota(jnp.int32, (8, width), 1)
    for to in range(peers):
        first = (2 * (to % row_tasks) + core) * blocks
        own = total[pl.ds(first, blocks), pl.ds(to // row_tasks * pairs, pairs), :]
        value = (own + other[to]).reshape(rows, width)
        largest = jnp.maximum(jnp.max(jnp.abs(value), axis=1, keepdims=True), FLOOR)
        level = jnp.floor(jnp.log2(largest) * STEPS) + 2.0
        out[to, :rows] = jnp.round(value * (jnp.exp2(level * (-1.0 / STEPS)) * TOP)).astype(jnp.int32).astype(jnp.int16)
        scales = jnp.zeros(lane.shape, jnp.float32)
        for group in range(rows // 8):
            scales = jnp.where(lane == group, level[8 * group : 8 * group + 8], scales)
        out[to, rows:] = scales.astype(jnp.int32).astype(jnp.int16)


def decode_kernel(parts, out):
    pairs, width = out.shape[0], parts.shape[2]
    rows = parts.shape[1] - 8
    scales = [
        jnp.exp2(parts[source, rows:].astype(jnp.int32).astype(jnp.float32) * (1.0 / STEPS)) * (1.0 / TOP)
        for source in range(parts.shape[0])
    ]
    for group in range(rows // 8):
        first = 8 * group
        total = jnp.zeros((8, width), jnp.float32)
        for source, scale in enumerate(scales):
            value = parts[source, first : first + 8].astype(jnp.int32).astype(jnp.float32)
            total += value * scale[:, group : group + 1]
        out[first % pairs : first % pairs + 8, first // pairs * width : (first // pairs + 1) * width] = total


def body(amplitudes, integral_tiles, task_list, block_offsets, tile_counts, *, shape):
    blocks, row_tasks = shape
    tasks = 2 * row_tasks
    chunk, span, pair_total = amplitudes.shape
    row_block = integral_tiles.shape[5]
    slots = blocks * tasks
    piece = chunk // tasks
    rows, pairs = NRB // tasks, pair_total // blocks
    core = lax.axis_index("core").astype(jnp.int32)
    ty = lax.axis_index("ty").astype(jnp.int32)
    worker = ty * 2 + core

    sent = pack(integral_tiles, tile_counts, blocks).reshape(slots, chunk + piece, row_block)
    arrived = lax.all_to_all(sent, EVERY, 0, 0, tiled=True)

    lists = lax.all_gather(task_list * NRB + block_offsets, TASK, axis=1, tiled=True)
    counts, lists = lax.optimization_barrier((tile_counts[:, 0], lists))
    mine = lax.dynamic_index_in_dim(lists, worker, 2, keepdims=False)
    second_row = jnp.sum(jnp.where(counts[:, None] == 2, lists[..., 1] % NRB, 0), axis=-1)
    meta = jnp.concatenate([(mine[..., 0] % NRB).reshape(-1), second_row.reshape(-1), core[None]])

    owner = lax.dynamic_index_in_dim(counts, worker, 1) == 2
    column = jnp.where(owner, mine[..., 1] // NRB, span).reshape(-1)
    first = (mine[..., 0] // NRB).reshape(-1)
    others = []
    for hop in range(1, row_tasks):
        there, here = pick(column, amplitudes, hop, row_tasks, slots)
        away = here + lax.ppermute(there, "core", [(0, 1), (1, 0)])
        others.append(lax.ppermute(away, "ty", [(i, (i + hop) % row_tasks) for i in range(row_tasks)]))
        column, first, _ = lax.optimization_barrier((column, first, away))
    if piece % 16:
        there, here = pick(column, amplitudes, 0, row_tasks, slots)
        hot = (first[:, None] == jnp.arange(span, dtype=jnp.int32)).astype(amplitudes.dtype)
        columns = jnp.einsum("nd,cdp->ncp", hot, amplitudes)
    else:
        there, here, columns = pick(jnp.concatenate([column, first]), amplitudes, 0, row_tasks, slots)
    others.append(lax.ppermute(there, "core", [(0, 1), (1, 0)]))
    extras = sum(others, here)

    part = jax.ShapeDtypeStruct((blocks, row_tasks, rows, pairs, row_block), jnp.float32)
    in_vmem = pl.BlockSpec(memory_space=pltpu.VMEM)
    send, total = pl.pallas_call(
        functools.partial(ladder_kernel, row_tasks=row_tasks, pair_blocks=blocks),
        out_shape=(part, jax.ShapeDtypeStruct((NRB, pair_total, row_block), jnp.float32)),
        in_specs=[pl.BlockSpec(memory_space=pltpu.SMEM)] + [in_vmem] * 3,
        out_specs=(in_vmem, in_vmem),
        compiler_params=pltpu.CompilerParams(vmem_limit_bytes=16 << 20),
        cost_estimate=pl.CostEstimate(
            flops=2 * slots * (chunk + piece) * pair_total * row_block,
            bytes_accessed=2 * slots * (chunk + piece) * (pair_total + row_block) + 4 * NRB * pair_total * row_block,
            transcendentals=0,
        ),
        name="ladder",
    )(meta, columns, arrived, extras)

    other = lax.ppermute(send, "core", [(0, 1), (1, 0)])
    peers = blocks * row_tasks
    cut = (peers, rows, pairs, row_block)
    coded = pl.pallas_call(
        functools.partial(code_kernel, row_tasks=row_tasks),
        out_shape=jax.ShapeDtypeStruct((peers, rows * pairs + 8, row_block), jnp.int16),
        in_specs=[in_vmem, in_vmem],
        out_specs=in_vmem,
        compiler_params=pltpu.CompilerParams(vmem_limit_bytes=16 << 20),
        name="code",
    )(total, other.reshape(cut))
    parts = lax.all_to_all(coded, ("blk", "ty"), 0, 0, tiled=True)
    return pl.pallas_call(
        decode_kernel,
        out_shape=jax.ShapeDtypeStruct((pairs, rows * row_block), jnp.float32),
        in_specs=[in_vmem],
        out_specs=in_vmem,
        compiler_params=pltpu.CompilerParams(vmem_limit_bytes=16 << 20),
        name="decode",
    )(parts)


def solution(mesh):
    blocks, tasks = mesh.shape["blk"], mesh.shape["task"]
    fine = Mesh(mesh.devices.reshape(blocks, tasks // 2, 2), EVERY)
    placed = (
        P("blk", TASK, None),
        P("blk", TASK, None, None, None, None),
        P(None, TASK, None, None),
        P(None, TASK, None, None),
        P(None, TASK, None),
    )
    return jax.shard_map(
        functools.partial(body, shape=(blocks, tasks // 2)),
        mesh=fine, in_specs=placed, out_specs=P("blk", TASK), check_vma=False,
    )
```

```python
import functools

import jax
import jax.numpy as jnp
from jax import lax
from jax.experimental import pallas as pl
from jax.experimental.pallas import tpu as pltpu
from jax.sharding import Mesh, PartitionSpec as P

NRB = 16
TASK = ("ty", "core")
BLK = ("z", "x")
AXES = BLK + TASK
EVERY = ("x", "ty", "core", "z")


def pack_kernel(counts, tiles, pieces, out, held, busy, in_sem, out_sem, count_sem):
    tasks, _, _, rows, _ = held.shape
    chunk = tiles.shape[3]
    upper, lower = pl.ds(0, chunk), pl.ds(chunk, rows - chunk)
    count_copy = pltpu.make_async_copy(counts, busy, count_sem)
    count_copy.start()
    first = [pltpu.make_async_copy(tiles.at[2 * w], held.at[w, :, :, upper], in_sem.at[0, w]) for w in range(tasks)]
    for copy in first:
        copy.start()
    count_copy.wait()
    group = 2 * lax.axis_index("z") + lax.axis_index("x")
    tile = 1
    for w in range(1, tasks):
        tile = jnp.where(busy[w, group] == 2, 2 * w + 1, tile)
    second = [
        pltpu.make_async_copy(pieces.at[tile, :, :, w], held.at[w, :, :, lower], in_sem.at[1, w]) for w in range(tasks)
    ]
    for copy in second:
        copy.start()
    leave = [
        [
            pltpu.make_async_copy(held.at[w, :, x, span], out.at[x, w, :, span], out_sem.at[half, w, x])
            for x in range(2)
        ]
        for half, span in enumerate((upper, lower))
        for w in range(tasks)
    ]
    for arrive, go in zip(first + second, leave):
        arrive.wait()
        for copy in go:
            copy.start()
    leave = sum(leave, [])
    for copy in leave:
        copy.wait()


def pack(integral_tiles, tile_counts, blocks):
    tasks, _, virt_total, row_block = integral_tiles.shape[2:]
    chunk = virt_total // blocks
    piece = chunk // tasks
    tiles = integral_tiles.reshape(tasks * 2, blocks // 2, 2, chunk, row_block)
    pieces = integral_tiles.reshape(tasks * 2, blocks // 2, 2, tasks, piece, row_block)
    counts = jnp.transpose(tile_counts[:, 0])
    if piece % 16:
        own = lax.dynamic_index_in_dim(counts, lax.axis_index(BLK), 1, keepdims=False)
        second = lax.dynamic_index_in_dim(pieces, 2 * jnp.argmax(own) + 1, 0, keepdims=False)
        return jnp.concatenate([jnp.transpose(tiles[::2], (2, 0, 1, 3, 4)), jnp.transpose(second, (1, 2, 0, 3, 4))], axis=3)
    return pl.pallas_call(
        pack_kernel,
        out_shape=jax.ShapeDtypeStruct((2, tasks, blocks // 2, chunk + piece, row_block), tiles.dtype),
        in_specs=[pl.BlockSpec(memory_space=pl.ANY)] * 3,
        out_specs=pl.BlockSpec(memory_space=pl.ANY),
        scratch_shapes=[
            pltpu.VMEM((tasks, blocks // 2, 2, chunk + piece, row_block), tiles.dtype),
            pltpu.SMEM(counts.shape, counts.dtype),
        ]
        + [pltpu.SemaphoreType.DMA((2, tasks)), pltpu.SemaphoreType.DMA((2, tasks, 2))]
        + [pltpu.SemaphoreType.DMA],
        compiler_params=pltpu.CompilerParams(vmem_limit_bytes=58 << 20),
        name="pack",
    )(counts, tiles, pieces)


def pick_kernel(lists, amplitudes, there, here, *refs, hop, row_tasks):
    columns = refs[0] if len(refs) == 5 else None
    held, hot, picked, sems = refs[-4:]
    slots, piece, _ = here.shape
    sides, parts = sems.shape
    rows = piece // parts
    core, row_task = lax.axis_index("core"), lax.axis_index("ty") + hop

    def base_of(side):
        task = 2 * lax.rem(row_task + side // 2, row_tasks) + lax.rem(core + 1 + side, 2)
        return pl.multiple_of(task * piece, piece)

    def copy_of(side, part):
        return pltpu.make_async_copy(
            amplitudes.at[pl.ds(base_of(side) + part * rows, rows)],
            held.at[side, pl.ds(part * rows, rows)],
            sems.at[side, part],
        )

    for side in range(sides):
        for part in range(parts):
            copy_of(side, part).start()

    lane = lax.broadcasted_iota(jnp.int32, (1, hot.shape[1]), 1)
    for n in range(hot.shape[0]):
        hot[pl.ds(n, 1), :] = jnp.where(lane == lists[n], 1.0, 0.0)
    chosen = hot[...].astype(held.dtype)

    for side in range(sides):
        for part in range(parts):
            copy_of(side, part).wait()
            for c in range(part * rows, (part + 1) * rows):
                picked[c] = jnp.dot(chosen, held[side, c], preferred_element_type=jnp.float32)
        if side < 2:
            for n in range(slots):
                (there, here)[side][n] = picked[:, n, :].astype(here.dtype)
        if columns is not None:
            for n in range(slots):
                columns[n, pl.ds(base_of(side), piece), :] = picked[:, slots + n, :].astype(columns.dtype)


def pick(lists, amplitudes, hop, row_tasks, slots):
    chunk, span, pair_total = amplitudes.shape
    tasks = 2 * row_tasks
    piece = chunk // tasks
    listed = lists.shape[0]
    sides = tasks if listed > slots else 2
    part = jax.ShapeDtypeStruct((slots, piece, pair_total), amplitudes.dtype)
    whole = jax.ShapeDtypeStruct((slots, chunk, pair_total), amplitudes.dtype)
    outs = (part, part, whole) if listed > slots else (part, part)
    return pl.pallas_call(
        functools.partial(pick_kernel, hop=hop, row_tasks=row_tasks),
        out_shape=outs,
        in_specs=[pl.BlockSpec(memory_space=pltpu.SMEM), pl.BlockSpec(memory_space=pl.ANY)],
        out_specs=(pl.BlockSpec(memory_space=pltpu.VMEM),) * len(outs),
        scratch_shapes=[
            pltpu.VMEM((sides, piece, span, pair_total), amplitudes.dtype),
            pltpu.VMEM((listed, span), jnp.float32),
            pltpu.VMEM((piece, listed, pair_total), jnp.float32),
            pltpu.SemaphoreType.DMA((sides, 4)),
        ],
        compiler_params=pltpu.CompilerParams(vmem_limit_bytes=48 << 20),
        cost_estimate=pl.CostEstimate(
            flops=2 * listed * sides * piece * span * pair_total,
            bytes_accessed=2 * sides * piece * (span + listed) * pair_total,
            transcendentals=0,
        ),
        name="pick",
    )(lists, amplitudes)


def dot_rows(left, right):
    return lax.dot_general(left, right, (((0,), (0,)), ((), ())), preferred_element_type=jnp.float32)


def ladder_kernel(meta, columns, tiles, extras, send, total, *, row_tasks, pair_blocks):
    slots, chunk, _ = columns.shape
    total[...] = jnp.zeros_like(total)

    group = min(slots, 32)

    def add_slots(step, carry):
        for part in range(group):
            n = step * group + part
            total[meta[n]] += dot_rows(columns[n], tiles[n, :chunk])
            total[meta[slots + n]] += dot_rows(extras[n], tiles[n, chunk:])
        return carry

    lax.fori_loop(0, slots // group, add_slots, 0)

    core = meta[2 * slots]
    rows = NRB // (2 * row_tasks)
    pairs = total.shape[1] // pair_blocks
    for task in range(row_tasks):
        for block in range(pair_blocks):
            span = pl.ds(block * pairs, pairs)
            for row in range(rows):
                send[block, task, row] = total[(2 * task + 1 - core) * rows + row, span, :]


STEPS, TOP, FLOOR = 64.0, 32752.0, 2.0**-111


def code_kernel(total, other, out, *, row_tasks):
    peers, blocks, pairs, width = other.shape
    rows = blocks * pairs
    core = lax.axis_index("core")
    lane = lax.broadcasted_iota(jnp.int32, (8, width), 1)
    for to in range(peers):
        first = (2 * (to % row_tasks) + core) * blocks
        own = total[pl.ds(first, blocks), pl.ds(to // row_tasks * pairs, pairs), :]
        value = (own + other[to]).reshape(rows, width)
        largest = jnp.maximum(jnp.max(jnp.abs(value), axis=1, keepdims=True), FLOOR)
        level = jnp.floor(jnp.log2(largest) * STEPS) + 2.0
        out[to, :rows] = jnp.round(value * (jnp.exp2(level * (-1.0 / STEPS)) * TOP)).astype(jnp.int32).astype(jnp.int16)
        scales = jnp.zeros(lane.shape, jnp.float32)
        for group in range(rows // 8):
            scales = jnp.where(lane == group, level[8 * group : 8 * group + 8], scales)
        out[to, rows:] = scales.astype(jnp.int32).astype(jnp.int16)


def decode_kernel(parts, out):
    pairs, width = out.shape[0], parts.shape[2]
    rows = parts.shape[1] - 8
    scales = [
        jnp.exp2(parts[source, rows:].astype(jnp.int32).astype(jnp.float32) * (1.0 / STEPS)) * (1.0 / TOP)
        for source in range(parts.shape[0])
    ]
    for group in range(rows // 8):
        first = 8 * group
        total = jnp.zeros((8, width), jnp.float32)
        for source, scale in enumerate(scales):
            value = parts[source, first : first + 8].astype(jnp.int32).astype(jnp.float32)
            total += value * scale[:, group : group + 1]
        out[first % pairs : first % pairs + 8, first // pairs * width : (first // pairs + 1) * width] = total


def body(amplitudes, integral_tiles, task_list, block_offsets, tile_counts, *, shape):
    blocks, row_tasks = shape
    tasks = 2 * row_tasks
    chunk, span, pair_total = amplitudes.shape
    row_block = integral_tiles.shape[5]
    slots = blocks * tasks
    piece = chunk // tasks
    rows, pairs = NRB // tasks, pair_total // blocks
    core = lax.axis_index("core").astype(jnp.int32)
    ty = lax.axis_index("ty").astype(jnp.int32)
    worker = ty * 2 + core

    sent = pack(integral_tiles, tile_counts, blocks).reshape(slots, chunk + piece, row_block)
    arrived = lax.all_to_all(sent, EVERY, 0, 0, tiled=True)

    lists = lax.all_gather(task_list * NRB + block_offsets, TASK, axis=1, tiled=True)
    counts, lists = lax.optimization_barrier((tile_counts[:, 0], lists))
    mine = lax.dynamic_index_in_dim(lists, worker, 2, keepdims=False)
    second_row = jnp.sum(jnp.where(counts[:, None] == 2, lists[..., 1] % NRB, 0), axis=-1)


    def in_order(table):
        return jnp.transpose(table.reshape(blocks // 2, 2, tasks), (1, 2, 0)).reshape(-1)

    meta = jnp.concatenate([in_order(mine[..., 0] % NRB), in_order(second_row), core[None]])

    owner = lax.dynamic_index_in_dim(counts, worker, 1) == 2
    column = in_order(jnp.where(owner, mine[..., 1] // NRB, span))
    first = in_order(mine[..., 0] // NRB)
    others = []
    for hop in range(1, row_tasks):
        there, here = pick(column, amplitudes, hop, row_tasks, slots)
        away = here + lax.ppermute(there, "core", [(0, 1), (1, 0)])
        others.append(lax.ppermute(away, "ty", [(i, (i + hop) % row_tasks) for i in range(row_tasks)]))
        column, first, _ = lax.optimization_barrier((column, first, away))
    if piece % 16:
        there, here = pick(column, amplitudes, 0, row_tasks, slots)
        hot = (first[:, None] == jnp.arange(span, dtype=jnp.int32)).astype(amplitudes.dtype)
        columns = jnp.einsum("nd,cdp->ncp", hot, amplitudes)
    else:
        there, here, columns = pick(jnp.concatenate([column, first]), amplitudes, 0, row_tasks, slots)
    others.append(lax.ppermute(there, "core", [(0, 1), (1, 0)]))
    extras = sum(others, here)

    part = jax.ShapeDtypeStruct((blocks, row_tasks, rows, pairs, row_block), jnp.float32)
    in_vmem = pl.BlockSpec(memory_space=pltpu.VMEM)
    send, total = pl.pallas_call(
        functools.partial(ladder_kernel, row_tasks=row_tasks, pair_blocks=blocks),
        out_shape=(part, jax.ShapeDtypeStruct((NRB, pair_total, row_block), jnp.float32)),
        in_specs=[pl.BlockSpec(memory_space=pltpu.SMEM)] + [in_vmem] * 3,
        out_specs=(in_vmem, in_vmem),
        compiler_params=pltpu.CompilerParams(vmem_limit_bytes=16 << 20),
        cost_estimate=pl.CostEstimate(
            flops=2 * slots * (chunk + piece) * pair_total * row_block,
            bytes_accessed=2 * slots * (chunk + piece) * (pair_total + row_block) + 4 * NRB * pair_total * row_block,
            transcendentals=0,
        ),
        name="ladder",
    )(meta, columns, arrived, extras)

    other = lax.ppermute(send, "core", [(0, 1), (1, 0)])
    peers = blocks * row_tasks
    cut = (peers, rows, pairs, row_block)
    coded = pl.pallas_call(
        functools.partial(code_kernel, row_tasks=row_tasks),
        out_shape=jax.ShapeDtypeStruct((peers, rows * pairs + 8, row_block), jnp.int16),
        in_specs=[in_vmem, in_vmem],
        out_specs=in_vmem,
        compiler_params=pltpu.CompilerParams(vmem_limit_bytes=16 << 20),
        name="code",
    )(total, other.reshape(cut))
    parts = lax.all_to_all(coded, BLK + ("ty",), 0, 0, tiled=True)
    return pl.pallas_call(
        decode_kernel,
        out_shape=jax.ShapeDtypeStruct((pairs, rows * row_block), jnp.float32),
        in_specs=[in_vmem],
        out_specs=in_vmem,
        compiler_params=pltpu.CompilerParams(vmem_limit_bytes=16 << 20),
        name="decode",
    )(parts)


def solution(mesh):
    blocks, tasks = mesh.shape["blk"], mesh.shape["task"]
    fine = Mesh(mesh.devices.reshape(blocks // 2, 2, tasks // 2, 2), AXES)
    placed = (
        P(BLK, TASK, None),
        P(BLK, TASK, None, None, None, None),
        P(None, TASK, None, None),
        P(None, TASK, None, None),
        P(None, TASK, None),
    )
    return jax.shard_map(
        functools.partial(body, shape=(blocks, tasks // 2)),
        mesh=fine, in_specs=placed, out_specs=P(BLK, TASK), check_vma=False,
    )
```

```python
import functools

import jax
import jax.numpy as jnp
from jax import lax
from jax.experimental import pallas as pl
from jax.experimental.pallas import tpu as pltpu
from jax.sharding import Mesh, PartitionSpec as P

NRB = 16
TASK = ("ty", "core")
BLK = ("z", "x")
AXES = BLK + TASK
EVERY = ("x", "ty", "core", "z")


def pack_kernel(counts, tiles, pieces, out, held, cut, busy, in_sem, out_sem, count_sem):
    tasks, _, _, chunk, _ = held.shape
    rows = out.shape[3]
    upper, lower = pl.ds(0, chunk), pl.ds(chunk, rows - chunk)
    count_copy = pltpu.make_async_copy(counts, busy, count_sem)
    count_copy.start()
    first = [pltpu.make_async_copy(tiles.at[2 * w], held.at[w], in_sem.at[0, w, 0]) for w in range(tasks)]
    for copy in first:
        copy.start()
    count_copy.wait()
    group = 2 * lax.axis_index("z") + lax.axis_index("x")
    tile = 1
    for w in range(1, tasks):
        tile = jnp.where(busy[w, group] == 2, 2 * w + 1, tile)
    second = [
        pltpu.make_async_copy(pieces.at[tile, :, x, w], cut.at[x, w], in_sem.at[1, w, x])
        for w in range(tasks)
        for x in range(2)
    ]
    for copy in second:
        copy.start()
    leave = []
    for w, copy in enumerate(first):
        copy.wait()
        for x in range(2):
            leave.append(pltpu.make_async_copy(held.at[w, :, x], out.at[x, w, :, upper], out_sem.at[0, w, x]))
            leave[-1].start()
    for copy in second:
        copy.wait()
    leave.append(pltpu.make_async_copy(cut, out.at[:, :, :, lower], out_sem.at[1, 0, 0]))
    leave[-1].start()
    for copy in leave:
        copy.wait()


def pack(integral_tiles, tile_counts, blocks):
    tasks, _, virt_total, row_block = integral_tiles.shape[2:]
    chunk = virt_total // blocks
    piece = chunk // tasks
    tiles = integral_tiles.reshape(tasks * 2, blocks // 2, 2, chunk, row_block)
    pieces = integral_tiles.reshape(tasks * 2, blocks // 2, 2, tasks, piece, row_block)
    counts = jnp.transpose(tile_counts[:, 0])
    if piece % 16:
        own = lax.dynamic_index_in_dim(counts, lax.axis_index(BLK), 1, keepdims=False)
        second = lax.dynamic_index_in_dim(pieces, 2 * jnp.argmax(own) + 1, 0, keepdims=False)
        return jnp.concatenate([jnp.transpose(tiles[::2], (2, 0, 1, 3, 4)), jnp.transpose(second, (1, 2, 0, 3, 4))], axis=3)
    return pl.pallas_call(
        pack_kernel,
        out_shape=jax.ShapeDtypeStruct((2, tasks, blocks // 2, chunk + piece, row_block), tiles.dtype),
        in_specs=[pl.BlockSpec(memory_space=pl.ANY)] * 3,
        out_specs=pl.BlockSpec(memory_space=pl.ANY),
        scratch_shapes=[
            pltpu.VMEM((tasks, blocks // 2, 2, chunk, row_block), tiles.dtype),
            pltpu.VMEM((2, tasks, blocks // 2, piece, row_block), tiles.dtype),
            pltpu.SMEM(counts.shape, counts.dtype),
        ]
        + [pltpu.SemaphoreType.DMA((2, tasks, 2))] * 2
        + [pltpu.SemaphoreType.DMA],
        compiler_params=pltpu.CompilerParams(vmem_limit_bytes=58 << 20),
        name="pack",
    )(counts, tiles, pieces)


def pick_kernel(lists, amplitudes, there, here, *refs, hop, row_tasks):
    columns = refs[0] if len(refs) == 5 else None
    held, hot, picked, sems = refs[-4:]
    slots, piece, _ = here.shape
    sides, parts = sems.shape
    rows = piece // parts
    core, row_task = lax.axis_index("core"), lax.axis_index("ty") + hop

    def base_of(side):
        task = 2 * lax.rem(row_task + side // 2, row_tasks) + lax.rem(core + 1 + side, 2)
        return pl.multiple_of(task * piece, piece)

    def copy_of(side, part):
        return pltpu.make_async_copy(
            amplitudes.at[pl.ds(base_of(side) + part * rows, rows)],
            held.at[side, pl.ds(part * rows, rows)],
            sems.at[side, part],
        )

    for side in range(sides):
        for part in range(parts):
            copy_of(side, part).start()

    lane = lax.broadcasted_iota(jnp.int32, (1, hot.shape[1]), 1)
    for n in range(hot.shape[0]):
        hot[pl.ds(n, 1), :] = jnp.where(lane == lists[n], 1.0, 0.0)
    chosen = hot[...].astype(held.dtype)

    for side in range(sides):
        for part in range(parts):
            copy_of(side, part).wait()
            for c in range(part * rows, (part + 1) * rows):
                picked[c] = jnp.dot(chosen, held[side, c], preferred_element_type=jnp.float32)
        if side < 2:
            for n in range(slots):
                (there, here)[side][n] = picked[:, n, :].astype(here.dtype)
        if columns is not None:
            for n in range(slots):
                columns[n, pl.ds(base_of(side), piece), :] = picked[:, slots + n, :].astype(columns.dtype)


def pick(lists, amplitudes, hop, row_tasks, slots):
    chunk, span, pair_total = amplitudes.shape
    tasks = 2 * row_tasks
    piece = chunk // tasks
    listed = lists.shape[0]
    sides = tasks if listed > slots else 2
    part = jax.ShapeDtypeStruct((slots, piece, pair_total), amplitudes.dtype)
    whole = jax.ShapeDtypeStruct((slots, chunk, pair_total), amplitudes.dtype)
    outs = (part, part, whole) if listed > slots else (part, part)
    return pl.pallas_call(
        functools.partial(pick_kernel, hop=hop, row_tasks=row_tasks),
        out_shape=outs,
        in_specs=[pl.BlockSpec(memory_space=pltpu.SMEM), pl.BlockSpec(memory_space=pl.ANY)],
        out_specs=(pl.BlockSpec(memory_space=pltpu.VMEM),) * len(outs),
        scratch_shapes=[
            pltpu.VMEM((sides, piece, span, pair_total), amplitudes.dtype),
            pltpu.VMEM((listed, span), jnp.float32),
            pltpu.VMEM((piece, listed, pair_total), jnp.float32),
            pltpu.SemaphoreType.DMA((sides, 4)),
        ],
        compiler_params=pltpu.CompilerParams(vmem_limit_bytes=48 << 20),
        cost_estimate=pl.CostEstimate(
            flops=2 * listed * sides * piece * span * pair_total,
            bytes_accessed=2 * sides * piece * (span + listed) * pair_total,
            transcendentals=0,
        ),
        name="pick",
    )(lists, amplitudes)


def dot_rows(left, right):
    return lax.dot_general(left, right, (((0,), (0,)), ((), ())), preferred_element_type=jnp.float32)


def ladder_kernel(meta, columns, tiles, extras, send, total, *, row_tasks, pair_blocks):
    slots, chunk, _ = columns.shape
    total[...] = jnp.zeros_like(total)

    group = min(slots, 32)

    def add_slots(step, carry):
        for part in range(group):
            n = step * group + part
            total[meta[n]] += dot_rows(columns[n], tiles[n, :chunk])
            total[meta[slots + n]] += dot_rows(extras[n], tiles[n, chunk:])
        return carry

    lax.fori_loop(0, slots // group, add_slots, 0)

    core = meta[2 * slots]
    rows = NRB // (2 * row_tasks)
    pairs = total.shape[1] // pair_blocks
    for task in range(row_tasks):
        for block in range(pair_blocks):
            span = pl.ds(block * pairs, pairs)
            for row in range(rows):
                send[block, task, row] = total[(2 * task + 1 - core) * rows + row, span, :]


STEPS, TOP, FLOOR = 64.0, 32752.0, 2.0**-111


def code_kernel(total, other, out, *, row_tasks):
    peers, blocks, pairs, width = other.shape
    rows = blocks * pairs
    core = lax.axis_index("core")
    lane = lax.broadcasted_iota(jnp.int32, (8, width), 1)
    for to in range(peers):
        first = (2 * (to % row_tasks) + core) * blocks
        own = total[pl.ds(first, blocks), pl.ds(to // row_tasks * pairs, pairs), :]
        value = (own + other[to]).reshape(rows, width)
        largest = jnp.maximum(jnp.max(jnp.abs(value), axis=1, keepdims=True), FLOOR)
        level = jnp.floor(jnp.log2(largest) * STEPS) + 2.0
        out[to, :rows] = jnp.round(value * (jnp.exp2(level * (-1.0 / STEPS)) * TOP)).astype(jnp.int32).astype(jnp.int16)
        scales = jnp.zeros(lane.shape, jnp.float32)
        for group in range(rows // 8):
            scales = jnp.where(lane == group, level[8 * group : 8 * group + 8], scales)
        out[to, rows:] = scales.astype(jnp.int32).astype(jnp.int16)


def decode_kernel(parts, out):
    pairs, width = out.shape[0], parts.shape[2]
    rows = parts.shape[1] - 8
    scales = [
        jnp.exp2(parts[source, rows:].astype(jnp.int32).astype(jnp.float32) * (1.0 / STEPS)) * (1.0 / TOP)
        for source in range(parts.shape[0])
    ]
    for group in range(rows // 8):
        first = 8 * group
        total = jnp.zeros((8, width), jnp.float32)
        for source, scale in enumerate(scales):
            value = parts[source, first : first + 8].astype(jnp.int32).astype(jnp.float32)
            total += value * scale[:, group : group + 1]
        out[first % pairs : first % pairs + 8, first // pairs * width : (first // pairs + 1) * width] = total


def body(amplitudes, integral_tiles, task_list, block_offsets, tile_counts, *, shape):
    blocks, row_tasks = shape
    tasks = 2 * row_tasks
    chunk, span, pair_total = amplitudes.shape
    row_block = integral_tiles.shape[5]
    slots = blocks * tasks
    piece = chunk // tasks
    rows, pairs = NRB // tasks, pair_total // blocks
    core = lax.axis_index("core").astype(jnp.int32)
    ty = lax.axis_index("ty").astype(jnp.int32)
    worker = ty * 2 + core

    sent = pack(integral_tiles, tile_counts, blocks).reshape(slots, chunk + piece, row_block)
    arrived = lax.all_to_all(sent, EVERY, 0, 0, tiled=True)

    lists = lax.all_gather(task_list * NRB + block_offsets, TASK, axis=1, tiled=True)
    counts, lists = lax.optimization_barrier((tile_counts[:, 0], lists))
    mine = lax.dynamic_index_in_dim(lists, worker, 2, keepdims=False)
    second_row = jnp.sum(jnp.where(counts[:, None] == 2, lists[..., 1] % NRB, 0), axis=-1)


    def in_order(table):
        return jnp.transpose(table.reshape(blocks // 2, 2, tasks), (1, 2, 0)).reshape(-1)

    meta = jnp.concatenate([in_order(mine[..., 0] % NRB), in_order(second_row), core[None]])

    owner = lax.dynamic_index_in_dim(counts, worker, 1) == 2
    column = in_order(jnp.where(owner, mine[..., 1] // NRB, span))
    first = in_order(mine[..., 0] // NRB)
    others = []
    for hop in range(1, row_tasks):
        there, here = pick(column, amplitudes, hop, row_tasks, slots)
        away = here + lax.ppermute(there, "core", [(0, 1), (1, 0)])
        others.append(lax.ppermute(away, "ty", [(i, (i + hop) % row_tasks) for i in range(row_tasks)]))
        column, first, _ = lax.optimization_barrier((column, first, away))
    if piece % 16:
        there, here = pick(column, amplitudes, 0, row_tasks, slots)
        hot = (first[:, None] == jnp.arange(span, dtype=jnp.int32)).astype(amplitudes.dtype)
        columns = jnp.einsum("nd,cdp->ncp", hot, amplitudes)
    else:
        there, here, columns = pick(jnp.concatenate([column, first]), amplitudes, 0, row_tasks, slots)
    others.append(lax.ppermute(there, "core", [(0, 1), (1, 0)]))
    extras = sum(others, here)

    part = jax.ShapeDtypeStruct((blocks, row_tasks, rows, pairs, row_block), jnp.float32)
    in_vmem = pl.BlockSpec(memory_space=pltpu.VMEM)
    send, total = pl.pallas_call(
        functools.partial(ladder_kernel, row_tasks=row_tasks, pair_blocks=blocks),
        out_shape=(part, jax.ShapeDtypeStruct((NRB, pair_total, row_block), jnp.float32)),
        in_specs=[pl.BlockSpec(memory_space=pltpu.SMEM)] + [in_vmem] * 3,
        out_specs=(in_vmem, in_vmem),
        compiler_params=pltpu.CompilerParams(vmem_limit_bytes=16 << 20),
        cost_estimate=pl.CostEstimate(
            flops=2 * slots * (chunk + piece) * pair_total * row_block,
            bytes_accessed=2 * slots * (chunk + piece) * (pair_total + row_block) + 4 * NRB * pair_total * row_block,
            transcendentals=0,
        ),
        name="ladder",
    )(meta, columns, arrived, extras)

    other = lax.ppermute(send, "core", [(0, 1), (1, 0)])
    peers = blocks * row_tasks
    cut = (peers, rows, pairs, row_block)
    coded = pl.pallas_call(
        functools.partial(code_kernel, row_tasks=row_tasks),
        out_shape=jax.ShapeDtypeStruct((peers, rows * pairs + 8, row_block), jnp.int16),
        in_specs=[in_vmem, in_vmem],
        out_specs=in_vmem,
        compiler_params=pltpu.CompilerParams(vmem_limit_bytes=16 << 20),
        name="code",
    )(total, other.reshape(cut))
    parts = lax.all_to_all(coded, BLK + ("ty",), 0, 0, tiled=True)
    return pl.pallas_call(
        decode_kernel,
        out_shape=jax.ShapeDtypeStruct((pairs, rows * row_block), jnp.float32),
        in_specs=[in_vmem],
        out_specs=in_vmem,
        compiler_params=pltpu.CompilerParams(vmem_limit_bytes=16 << 20),
        name="decode",
    )(parts)


def solution(mesh):
    blocks, tasks = mesh.shape["blk"], mesh.shape["task"]
    fine = Mesh(mesh.devices.reshape(blocks // 2, 2, tasks // 2, 2), AXES)
    placed = (
        P(BLK, TASK, None),
        P(BLK, TASK, None, None, None, None),
        P(None, TASK, None, None),
        P(None, TASK, None, None),
        P(None, TASK, None),
    )
    return jax.shard_map(
        functools.partial(body, shape=(blocks, tasks // 2)),
        mesh=fine, in_specs=placed, out_specs=P(BLK, TASK), check_vma=False,
    )
```
